512 devices in a mesh: row: 64 (over z, y), bundle: 8 (over x, core).
Axes of the slice: x: 4, y: 8, z: 8, core: 2. Of those that a mesh axis runs over, the one named last changes fastest.
Arguments:
- vectors: float32 [256, 131072], P('bundle', 'row'), may hold values from -6 to 6
- blocks: float32 [2048, 64, 384], P('row'), may hold values from -0.30618622 to 0.30618622, as said below
- columns: int32 [2048, 6], P('row'), may hold values from 0 to 2047, as said below
- bounds: float32 [2], replicated, may hold values from -0.9 to 0.5, as said below
Outputs:
- basis: float32 [256, 131072], P(None, ('row', 'bundle'))
- factor: float32 [256, 256], replicated
The draws below stay inside these ranges and needn't reach their ends.
Inputs may be any that keep to these rules, and one draw needn't show every extreme that they name: Slot 0 of block row i is i itself; every block column of block row i lies within 32 block rows of i, counted cyclically over the 2048 block rows, and a distance of exactly 32 occurs; columns of one block row may repeat. `blocks`: together with columns they make H symmetric. bounds[0] < 0 < bounds[1].
All inputs are finite; a program needn't handle non-finite values.
Results may differ from the reference program's by a relative error of at most 0.00011.
Values sent between devices are 32-bit elements; how exact they have to be, the bound alone decides.
No kernel may reach another device: no remote copies, remote signals or barrier semaphores. Data moves between devices by JAX's collectives and lax.ppermute only.
A program may use at most 64 MiB of HBM per device.

```python
import jax
import jax.numpy as jnp
from jax import lax

BS = 64
SLOTS = 6
K = 256
BR_DEV = 32
NBR = 2048
N = 131072


def pattern_tables(key):
    base = jax.random.fold_in(key, 101)
    rows = jnp.arange(NBR, dtype=jnp.int32)
    window = BR_DEV
    forward = []
    backward = []
    for pair_index in range(2):
        pair_key = jax.random.fold_in(base, pair_index)
        start = jax.random.randint(jax.random.fold_in(pair_key, 1), (), 0, window).astype(jnp.int32)
        turns = jax.random.randint(jax.random.fold_in(pair_key, 2), (NBR // window,), 1, window).astype(jnp.int32)
        position = jnp.mod(rows - start, NBR)
        which = position // window
        inner = position % window
        turn = turns[which]
        forward.append(jnp.mod(start + which * window + jnp.mod(inner + turn, window), NBR).astype(jnp.int32))
        backward.append(jnp.mod(start + which * window + jnp.mod(inner - turn, window), NBR).astype(jnp.int32))
    match_start = jax.random.randint(jax.random.fold_in(base, 7), (), 0, 2 * window).astype(jnp.int32)
    match_inner = jnp.mod(rows - match_start, NBR) % (2 * window)
    lower_half = match_inner < window
    partner = jnp.mod(rows + jnp.where(lower_half, window, -window), NBR).astype(jnp.int32)
    return (rows, forward, backward, partner, lower_half)


def draw_columns(key, part):
    rows, forward, backward, partner, lower_half = pattern_tables(key)
    return jnp.stack([rows, forward[0], backward[0], forward[1], backward[1], partner], axis=1).astype(jnp.int32)


def draw_blocks(key, part):
    rows, forward, backward, partner, lower_half = pattern_tables(key)
    sigma = (SLOTS * BS) ** (-0.5)
    raw_key = jax.random.fold_in(key, 211)
    raw = jnp.clip(jax.random.normal(raw_key, (NBR, SLOTS, BS, BS), jnp.float32), -6.0, 6.0) * sigma
    flip = lambda m: jnp.swapaxes(m, -1, -2)
    slot0 = 0.5 * (raw[:, 0] + flip(raw[:, 0]))
    slot1 = raw[:, 1]
    slot2 = flip(jnp.take(raw[:, 1], backward[0], axis=0))
    slot3 = raw[:, 3]
    slot4 = flip(jnp.take(raw[:, 3], backward[1], axis=0))
    slot5 = jnp.where(lower_half[:, None, None], raw[:, 5], flip(jnp.take(raw[:, 5], partner, axis=0)))
    stacked = jnp.stack([slot0, slot1, slot2, slot3, slot4, slot5], axis=1)
    return jnp.transpose(stacked, (0, 2, 1, 3)).reshape(NBR, BS, SLOTS * BS).astype(jnp.float32)


def draw_bounds(key, part):
    lower_end = jax.random.uniform(jax.random.fold_in(key, 31), (), jnp.float32, -0.9, -0.5)
    upper_end = jax.random.uniform(jax.random.fold_in(key, 37), (), jnp.float32, 0.1, 0.5)
    return jnp.stack([lower_end, upper_end]).astype(jnp.float32)


def shard_levels(rng, dims, shards, smallest, top_value):
    gain, own = 1.0, jax.random.fold_in(rng, 6)
    for dim, shards_of in shards:
        heights = jnp.exp(jax.random.uniform(jax.random.fold_in(own, dim), (shards_of,), jnp.float32, smallest / len(shards), top_value / len(shards)))
        gain = gain * jnp.repeat(heights, dims[dim] // shards_of).reshape([-1 if axis == dim else 1 for axis in range(len(dims))])
    return gain


def gaussian(stream_key, shape, spread, reach, shards=(), kind=jnp.bfloat16):
    drawn = spread * jax.random.normal(stream_key, shape, jnp.float32)
    if shards:
        drawn = drawn * shard_levels(stream_key, shape, shards, -0.22, 0.18)
    return jnp.clip(drawn, -reach, reach).astype(kind)


def setup_inputs(seed: int = 0) -> dict:
    splits = jax.random.split(jax.random.key(seed), 5)
    vectors = gaussian(splits[0], (K, N), 1.0, 6.0, ((0, 8), (1, 64)), jnp.float32)
    blocks = draw_blocks(jax.random.fold_in(splits[4], 71), 0)
    columns = draw_columns(jax.random.fold_in(splits[4], 71), 0)
    bounds = draw_bounds(jax.random.fold_in(splits[4], 71), 0)
    return {"vectors": vectors, "blocks": blocks, "columns": columns, "bounds": bounds}


def apply_operator(field, blocks, columns):
    width = field.shape[0]
    nblock = blocks.shape[0]
    field3 = field.reshape(width, nblock, BS)
    total = jnp.zeros((width, nblock, BS), jnp.float32)
    for slot in range(SLOTS):
        picked = jnp.take(field3, columns[:, slot], axis=1)
        piece = blocks[:, :, slot * BS:(slot + 1) * BS]
        total = total + jnp.einsum('iab,cib->cia', piece, picked, precision=lax.Precision.HIGHEST)
    return total.reshape(width, nblock * BS)

def reference(vectors, blocks, columns, bounds):
    center = (bounds[0] + bounds[1]) * 0.5
    half = (bounds[1] - bounds[0]) * 0.5
    first = (apply_operator(vectors, blocks, columns) - center * vectors) / half
    second = 2.0 * (apply_operator(first, blocks, columns) - center * first) / half - vectors
    filtered = 2.0 * (apply_operator(second, blocks, columns) - center * second) / half - first
    gram = jnp.dot(filtered.astype(jnp.float32), filtered.T.astype(jnp.float32), precision=lax.Precision.HIGHEST, preferred_element_type=jnp.float32)
    lower = jnp.linalg.cholesky(gram)
    basis = jax.scipy.linalg.solve_triangular(lower, filtered, lower=True)
    return (basis, lower.T)
```

```python
import functools

import jax
import jax.numpy as jnp
from jax import lax
from jax.experimental import pallas as pl
from jax.experimental.pallas import tpu as pltpu
from jax.sharding import PartitionSpec as P

BF = jnp.bfloat16
F32 = jnp.float32
HIGHEST = lax.Precision.HIGHEST
VMEM = pl.BlockSpec(memory_space=pltpu.VMEM)
SMEM = pl.BlockSpec(memory_space=pltpu.SMEM)
NB = 64
PIV = 4


def split(x):
    hi = x.astype(BF)
    lo = (x - hi.astype(F32)).astype(BF)
    return hi, lo


def dot_nt(a, b):
    return lax.dot_general(a, b, (((1,), (1,)), ((), ())), preferred_element_type=F32)


def split_kernel(b_ref, w_ref):
    hi, lo = split(b_ref[...])
    w_ref[:, 0:64, :] = hi
    w_ref[:, 64:128, :] = lo


def split_blocks(blocks):
    n, a, m = blocks.shape
    step = 8
    return pl.pallas_call(
        split_kernel,
        out_shape=jax.ShapeDtypeStruct((n, 2 * a, m), BF),
        grid=(n // step,),
        in_specs=[pl.BlockSpec((step, a, m), lambda i: (i, 0, 0))],
        out_specs=pl.BlockSpec((step, 2 * a, m), lambda i: (i, 0, 0)),
        name="split_blocks",
    )(blocks)


def apply_kernel(stage, total_rows, cols_ref, base_ref, bounds_ref, *refs):
    if stage == 0:
        f_ref, low_ref, high_ref, w_ref, out_ref, ehi, elo = refs
        prev_ref = None
    else:
        f_ref, low_ref, high_ref, prev_ref, w_ref, out_ref, ehi, elo = refs
    width = f_ref.shape[0]
    tiles = f_ref.shape[1] // 128

    for part, ref in enumerate((low_ref, f_ref, high_ref)):

        def build(t, carry, part=part, ref=ref):
            x = ref[:, pl.ds(pl.multiple_of(t * 128, 128), 128)]
            hi, lo = split(x)
            swapped = pltpu.roll(x, 64, 1)
            shi, slo = split(swapped)
            ehi[0, part * tiles + t] = hi
            elo[0, part * tiles + t] = lo
            ehi[1, part * tiles + t] = shi
            elo[1, part * tiles + t] = slo
            return carry

        lax.fori_loop(0, tiles, build, 0, unroll=4)

    base = base_ref[0]
    center = (bounds_ref[0] + bounds_ref[1]) * 0.5
    half = (bounds_ref[1] - bounds_ref[0]) * 0.5
    left_b = lax.broadcasted_iota(jnp.int32, (width, 128), 1) < 64
    slots = cols_ref.shape[1]

    def one(i):
        his, los = [], []
        for sp in range(slots // 2):
            ca = (cols_ref[i, 2 * sp] - base) & (total_rows - 1)
            cb = (cols_ref[i, 2 * sp + 1] - base) & (total_rows - 1)
            ta, va = ca >> 1, ca & 1
            tb, vb = cb >> 1, 1 - (cb & 1)
            his.append(jnp.where(left_b, ehi[va, ta], ehi[vb, tb]))
            los.append(jnp.where(left_b, elo[va, ta], elo[vb, tb]))
        lhs = jnp.concatenate(
            [jnp.concatenate(his, axis=1), jnp.concatenate(los, axis=1)], axis=0
        )
        out = dot_nt(lhs, w_ref[i])
        acc = out[:width] + jnp.where(left_b, out[width:], 0.0)
        return acc + pltpu.roll(acc, 64, 1)

    def pair(g, carry):
        y = jnp.where(left_b, one(2 * g), one(2 * g + 1))
        lanes = pl.ds(pl.multiple_of(g * 128, 128), 128)
        f = f_ref[:, lanes]
        r = (y - center * f) / half
        if stage > 0:
            r = 2.0 * r - prev_ref[:, lanes]
        if stage < 2:
            out_ref[:, lanes] = r
        else:
            out_ref[g] = r
        return carry

    lax.fori_loop(0, tiles, pair, 0, unroll=4)


def apply_step(stage, total_rows, cols, base, bounds, f, low, high, prev, w):
    width, n = f.shape
    tiles = n // 128
    args = (f, low, high) + (() if prev is None else (prev,)) + (w,)
    out = (width, n) if stage < 2 else (tiles, width, 128)
    return pl.pallas_call(
        functools.partial(apply_kernel, stage, total_rows),
        out_shape=jax.ShapeDtypeStruct(out, F32),
        in_specs=[SMEM] * 3 + [VMEM] * len(args),
        out_specs=VMEM,
        scratch_shapes=[pltpu.VMEM((2, 3 * tiles, width, 128), BF)] * 2,
        name=f"apply_{stage}",
    )(cols, base, bounds, *args)


def gram_kernel(s_ref, out_ref):
    s = jnp.concatenate(
        [
            s_ref[:, j].reshape(s_ref.shape[0] * s_ref.shape[2], 128)
            for j in range(s_ref.shape[1])
        ],
        axis=1,
    )
    g = lax.dot_general(
        s, s, (((1,), (1,)), ((), ())), precision=HIGHEST, preferred_element_type=F32
    )
    k = g.shape[0]
    for j in range(k // 128):
        out_ref[j] = g[:, j * 128 : (j + 1) * 128].reshape(k // 8, 8, 128)


def gram_tiles(s):
    k = s.shape[0] * s.shape[2]
    return pl.pallas_call(
        gram_kernel,
        out_shape=jax.ShapeDtypeStruct((k // 128, k // 8, 8, 128), F32),
        in_specs=[VMEM],
        out_specs=VMEM,
        name="gram",
    )(s)


def factor_block(m):
    n = m.shape[0]
    lane = lax.broadcasted_iota(jnp.int32, (8, 128), 1)
    sub = lax.broadcasted_iota(jnp.int32, (n, 128), 0)
    vregs = [m[8 * v : 8 * v + 8] for v in range(n // 8)]
    sub8 = lax.broadcasted_iota(jnp.int32, (8, 128), 0)
    done = [jnp.zeros((8, 128), F32) for _ in range(n // 8)]
    for j in range(0, n, PIV):
        v0 = j // 8
        rows = [
            jnp.broadcast_to(vregs[v0][j - 8 * v0 + k : j - 8 * v0 + k + 1, :], (8, 128))
            for k in range(PIV)
        ]
        p = {
            (k, c): jnp.broadcast_to(rows[k][:, j + c : j + c + 1], (8, 128))
            for k in range(PIV)
            for c in range(k, PIV)
        }
        cols = [
            [jnp.broadcast_to(vregs[v][:, j + c : j + c + 1], (8, 128)) for c in range(PIV)]
            for v in range(v0, n // 8)
        ]
        inv = []
        mult = {}
        for k in range(PIV):
            inv.append(1.0 / p[k, k])
            for r in range(k + 1, PIV):
                f = p[k, r] * inv[k]
                mult[r, k] = f
                for c in range(r, PIV):
                    p[r, c] = p[r, c] - f * p[k, c]
                rows[r] = rows[r] - f * rows[k]
        for k in range(PIV):
            u = rows[k] * lax.rsqrt(p[k, k])
            done[v0] = jnp.where(sub8 == j - 8 * v0 + k, u, done[v0])
        z = [rows[k] * inv[k] for k in range(PIV)]
        for k in range(PIV - 1, -1, -1):
            for r in range(k):
                z[r] = z[r] - mult[k, r] * z[k]
        for v in range(v0, n // 8):
            c = cols[v - v0]
            vregs[v] = vregs[v] - (
                (c[0] * z[0] + c[1] * z[1]) + (c[2] * z[2] + c[3] * z[3])
            )
    return jnp.concatenate(done, axis=0)


def solve_kernel(g_ref, s_ref, basis_ref, factor_ref, a_ref):
    k = factor_ref.shape[0]
    halves = k // 128
    for j in range(halves):
        a_ref[:, j * 128 : (j + 1) * 128] = g_ref[j].reshape(k, 128)
    for j in range(s_ref.shape[1]):
        a_ref[:, k + j * 128 : k + (j + 1) * 128] = s_ref[:, j].reshape(k, 128)
    total = a_ref.shape[1]
    lane = lax.broadcasted_iota(jnp.int32, (NB, 128), 1)
    sub = lax.broadcasted_iota(jnp.int32, (NB, 128), 0)
    eye = jnp.where(lane == sub + NB, 1.0, 0.0)

    def step(b, carry):
        first = pl.multiple_of(b * NB, NB)
        rows = pl.ds(first, NB)
        tile = a_ref[rows, pl.ds(pl.multiple_of((b // 2) * 128, 128), 128)]
        tile = jnp.where(b % 2 == 1, pltpu.roll(tile, NB, 1), tile)
        u = factor_block(jnp.where(lane < NB, tile, eye))
        linv = pltpu.roll(u, NB, 1)[:, :NB]
        x = lax.dot_general(
            linv,
            a_ref[rows, :],
            (((1,), (0,)), ((), ())),
            precision=HIGHEST,
            preferred_element_type=F32,
        )
        row_id = first + lax.broadcasted_iota(jnp.int32, (NB, k), 0)
        col_id = lax.broadcasted_iota(jnp.int32, (NB, k), 1)
        factor_ref[rows, :] = jnp.where(col_id >= row_id, x[:, :k], 0.0)
        basis_ref[rows, :] = x[:, k:]
        later = jnp.where(col_id >= first + NB, x[:, :k], 0.0)
        a_ref[...] -= lax.dot_general(
            later,
            x,
            (((0,), (0,)), ((), ())),
            precision=HIGHEST,
            preferred_element_type=F32,
        )
        return carry

    lax.fori_loop(0, k // NB, step, 0)


def orthonormalize(g, s):
    k = s.shape[0] * s.shape[2]
    n = s.shape[1] * 128
    return pl.pallas_call(
        solve_kernel,
        out_shape=(
            jax.ShapeDtypeStruct((k, n), F32),
            jax.ShapeDtypeStruct((k, k), F32),
        ),
        in_specs=[VMEM, VMEM],
        out_specs=(VMEM, VMEM),
        scratch_shapes=[pltpu.VMEM((k, k + n), F32)],
        name="orthonormalize",
    )(g, s)


def sum_over_devices(tiles):
    shape = tiles.shape
    rows = lax.axis_size("row")
    bundles = lax.axis_size("bundle")
    parts = lax.all_to_all(
        tiles.reshape(rows, -1, 128), "row", split_axis=0, concat_axis=0, tiled=True
    )
    mine = jnp.sum(parts, axis=0)
    parts = lax.all_to_all(
        jnp.broadcast_to(mine[None], (bundles,) + mine.shape),
        "bundle",
        split_axis=0,
        concat_axis=0,
        tiled=True,
    )
    mine = jnp.sum(parts, axis=0)
    parts = lax.all_to_all(
        jnp.broadcast_to(mine[None], (rows,) + mine.shape),
        "row",
        split_axis=0,
        concat_axis=0,
        tiled=True,
    )
    return parts.reshape(shape)


def local(vectors, blocks, columns, bounds):
    block_rows = blocks.shape[0]
    row_count = lax.axis_size("row")
    bundles = lax.axis_size("bundle")
    total_rows = block_rows * row_count
    base = ((lax.axis_index("row") - 1) * block_rows).astype(jnp.int32).reshape(1)
    forward = [(i, (i + 1) % row_count) for i in range(row_count)]
    backward = [(j, i) for i, j in forward]

    def sides(field):
        return (
            lax.ppermute(field, "row", forward),
            lax.ppermute(field, "row", backward),
        )

    low, high = sides(vectors)
    w = split_blocks(blocks)
    first = apply_step(
        0, total_rows, columns, base, bounds, vectors, low, high, None, w
    )
    low, high = sides(first)
    second = apply_step(
        1, total_rows, columns, base, bounds, first, low, high, vectors, w
    )
    low, high = sides(second)
    filtered = apply_step(
        2, total_rows, columns, base, bounds, second, low, high, first, w
    )
    tiles, width, lanes = filtered.shape
    stacked = lax.all_to_all(
        filtered.reshape(bundles, tiles // bundles, width, lanes),
        "bundle",
        split_axis=0,
        concat_axis=0,
        tiled=True,
    )
    gram = sum_over_devices(gram_tiles(stacked))
    return orthonormalize(gram, stacked)


def solution(mesh):
    placed = (P("bundle", "row"), P("row", None, None), P("row", None), P())
    return jax.shard_map(
        local,
        mesh=mesh,
        in_specs=placed,
        out_specs=(P(None, ("row", "bundle")), P()),
        check_vma=False,
    )
```

```python
import functools

import jax
import jax.numpy as jnp
from jax import lax
from jax.experimental import pallas as pl
from jax.experimental.pallas import tpu as pltpu
from jax.sharding import PartitionSpec as P

BF = jnp.bfloat16
F32 = jnp.float32
HIGHEST = lax.Precision.HIGHEST
VMEM = pl.BlockSpec(memory_space=pltpu.VMEM)
SMEM = pl.BlockSpec(memory_space=pltpu.SMEM)
NB = 64
BUILD_UNROLL = 8
PAIR_UNROLL = 8
PARAMS = pltpu.CompilerParams(vmem_limit_bytes=20 * 1024 * 1024)


def near(x):
    return pltpu.with_memory_space_constraint(x, pltpu.VMEM)


def split(x):
    hi = x.astype(BF)
    lo = (x - hi.astype(F32)).astype(BF)
    return hi, lo


def dot_nt(a, b):
    return lax.dot_general(a, b, (((1,), (1,)), ((), ())), preferred_element_type=F32)


def split_kernel(b_ref, w_ref):
    hi, lo = split(b_ref[...])
    w_ref[:, 0:64, :] = hi
    w_ref[:, 64:128, :] = lo


def split_blocks(blocks):
    n, a, m = blocks.shape
    step = 8
    return pl.pallas_call(
        split_kernel,
        out_shape=pltpu.VMEM((n, 2 * a, m), BF),
        grid=(n // step,),
        in_specs=[pl.BlockSpec((step, a, m), lambda i: (i, 0, 0))],
        out_specs=pl.BlockSpec((step, 2 * a, m), lambda i: (i, 0, 0)),
        compiler_params=PARAMS,
        name="split_blocks",
    )(blocks)


def apply_kernel(stage, slot_ref, bounds_ref, *refs):
    if stage == 0:
        f_ref, low_ref, high_ref, w_ref, out_ref, e_ref = refs
        prev_ref = None
    else:
        f_ref, low_ref, high_ref, prev_ref, w_ref, out_ref, e_ref = refs
    width = f_ref.shape[0]
    tiles = f_ref.shape[1] // 128
    left = lax.broadcasted_iota(jnp.int32, (width, 128), 1) < 64
    left2 = lax.broadcasted_iota(jnp.int32, (2 * width, 128), 1) < 64

    def build(t, carry):
        for part, ref in enumerate((low_ref, f_ref, high_ref)):
            x = ref[:, pl.ds(pl.multiple_of(t * 128, 128), 128)]
            for v, y in enumerate((x, pltpu.roll(x, 64, 1))):
                hi, lo = split(y)
                at = (3 * v + part) * tiles + t
                e_ref[at, 0:width] = hi
                e_ref[at, width : 2 * width] = lo
        return carry

    lax.fori_loop(0, tiles, build, 0, unroll=BUILD_UNROLL)

    center = (bounds_ref[0] + bounds_ref[1]) * 0.5
    half = (bounds_ref[1] - bounds_ref[0]) * 0.5
    slots = w_ref.shape[2] // 64

    def one(i):
        at = [slot_ref[i * slots + s] for s in range(slots)]
        lhs = jnp.concatenate(
            [
                jnp.where(left2, e_ref[at[s]], e_ref[at[s + 1]])
                for s in range(0, slots, 2)
            ],
            axis=1,
        )
        out = dot_nt(lhs, w_ref[i])
        acc = out[:width] + jnp.where(left, out[width:], 0.0)
        return acc + pltpu.roll(acc, 64, 1)

    def pair(g, carry):
        y = jnp.where(left, one(2 * g), one(2 * g + 1))
        lanes = pl.ds(pl.multiple_of(g * 128, 128), 128)
        f = f_ref[:, lanes]
        r = (y - center * f) / half
        if stage > 0:
            r = 2.0 * r - prev_ref[:, lanes]
        if stage < 2:
            out_ref[:, lanes] = r
        else:
            out_ref[g] = r
        return carry

    lax.fori_loop(0, tiles, pair, 0, unroll=PAIR_UNROLL)


def apply_step(stage, slot_table, bounds, f, low, high, prev, w):
    width, n = f.shape
    tiles = n // 128
    args = (f, low, high) + (() if prev is None else (prev,)) + (w,)
    out = (width, n) if stage < 2 else (tiles, width, 128)
    return pl.pallas_call(
        functools.partial(apply_kernel, stage),
        out_shape=pltpu.VMEM(out, F32),
        in_specs=[SMEM] * 2 + [VMEM] * len(args),
        out_specs=VMEM,
        scratch_shapes=[pltpu.VMEM((6 * tiles, 2 * width, 128), BF)],
        compiler_params=PARAMS,
        name=f"apply_{stage}",
    )(slot_table, bounds, *map(near, args))


def slot_places(columns, first_row, block_rows, total_rows):
    reach = jnp.mod(columns - first_row + block_rows, total_rows)
    right = jnp.arange(columns.shape[1], dtype=jnp.int32) % 2
    exchanged = (reach + right) % 2
    return (exchanged * (3 * block_rows // 2) + reach // 2).reshape(-1)


def gram_kernel(s_ref, out_ref):
    s = jnp.concatenate(
        [
            s_ref[:, j].reshape(s_ref.shape[0] * s_ref.shape[2], 128)
            for j in range(s_ref.shape[1])
        ],
        axis=1,
    )
    g = lax.dot_general(
        s, s, (((1,), (1,)), ((), ())), precision=HIGHEST, preferred_element_type=F32
    )
    k = g.shape[0]
    for j in range(k // 128):
        out_ref[j] = g[:, j * 128 : (j + 1) * 128].reshape(k // 8, 8, 128)


def gram_tiles(s):
    k = s.shape[0] * s.shape[2]
    return pl.pallas_call(
        gram_kernel,
        out_shape=pltpu.VMEM((k // 128, k // 8, 8, 128), F32),
        in_specs=[VMEM],
        out_specs=VMEM,
        compiler_params=PARAMS,
        name="gram",
    )(near(s))


def row_of(x, r):
    return jnp.broadcast_to(x[r : r + 1, :], (8, 128))


def lane_of(x, c):
    return jnp.broadcast_to(x[:, c : c + 1], (8, 128))


def factor_block(m):
    n = m.shape[0]
    sub = lax.broadcasted_iota(jnp.int32, (8, 128), 0)
    vregs = [m[8 * v : 8 * v + 8] for v in range(n // 8)]
    done = []
    for v0 in range(n // 8):
        head = vregs[v0]
        cols = [
            [lane_of(vregs[v], 8 * v0 + c) for c in range(8)]
            for v in range(v0, n // 8)
        ]
        rows = [row_of(head, k) for k in range(8)]
        p = {(k, c): row_of(cols[0][c], k) for c in range(8) for k in range(c + 1)}
        inv, mult = [], {}
        out = jnp.zeros((8, 128), F32)
        for k in range(8):
            inv.append(1.0 / p[k, k])
            for r in range(k + 1, 8):
                f = p[k, r] * inv[k]
                mult[k, r] = f
                for c in range(r, 8):
                    p[r, c] = p[r, c] - f * p[k, c]
                rows[r] = rows[r] - f * rows[k]
            out = jnp.where(sub == k, rows[k] * lax.rsqrt(p[k, k]), out)
        done.append(out)
        if v0 + 1 == n // 8:
            break
        z = [rows[k] * inv[k] for k in range(8)]
        for k in range(7, -1, -1):
            for r in range(k):
                z[r] = z[r] - mult[r, k] * z[k]
        for v in range(v0 + 1, n // 8):
            t = [cols[v - v0][k] * z[k] for k in range(8)]
            while len(t) > 1:
                t = [t[i] + t[i + 1] for i in range(0, len(t), 2)]
            vregs[v] = vregs[v] - t[0]
    return jnp.concatenate(done, axis=0)


def split3(x):
    a = x.astype(BF)
    r = x - a.astype(F32)
    b = r.astype(BF)
    c = (r - b.astype(F32)).astype(BF)
    return a, b, c


def six_lanes(twice):
    a, b, c = split3(twice)
    left = lax.broadcasted_iota(jnp.int32, twice.shape, 1) < NB
    return jnp.concatenate([a, jnp.where(left, b, a), jnp.where(left, b, c)], axis=1)


def six_rows(x):
    a, b, c = split3(x)
    return jnp.concatenate([a, b, a, c, b, a], axis=0)


def dot_nn(a, b):
    return lax.dot_general(a, b, (((1,), (0,)), ((), ())), preferred_element_type=F32)


def solve_kernel(g_ref, s_ref, basis_ref, factor_ref, a_ref):
    k = factor_ref.shape[0]
    halves = k // 128
    for j in range(halves):
        a_ref[:, j * 128 : (j + 1) * 128] = g_ref[j].reshape(k, 128)
    for j in range(s_ref.shape[1]):
        a_ref[:, k + j * 128 : k + (j + 1) * 128] = s_ref[:, j].reshape(k, 128)
    lane = lax.broadcasted_iota(jnp.int32, (NB, 128), 1)
    sub = lax.broadcasted_iota(jnp.int32, (NB, 128), 0)
    eye = jnp.where(lane == sub + NB, 1.0, 0.0)

    def step(b, carry):
        first = pl.multiple_of(b * NB, NB)
        rows = pl.ds(first, NB)
        tile = a_ref[rows, pl.ds(pl.multiple_of((b // 2) * 128, 128), 128)]
        tile = jnp.where(b % 2 == 1, pltpu.roll(tile, NB, 1), tile)
        u = factor_block(jnp.where(lane < NB, tile, eye))
        twice = jnp.where(lane < NB, pltpu.roll(u, NB, 1), u)
        x = dot_nn(six_lanes(twice), six_rows(a_ref[rows, :]))
        row_id = first + lax.broadcasted_iota(jnp.int32, (NB, k), 0)
        col_id = lax.broadcasted_iota(jnp.int32, (NB, k), 1)
        factor_ref[rows, :] = jnp.where(col_id >= row_id, x[:, :k], 0.0)
        basis_ref[rows, :] = x[:, k:]
        later = jnp.where(col_id >= first + NB, x[:, :k], 0.0)
        turned = jnp.concatenate([later, later], axis=0).T
        a_ref[...] -= dot_nn(six_lanes(turned), six_rows(x))
        return carry

    lax.fori_loop(0, k // NB, step, 0)


def orthonormalize(g, s):
    k = s.shape[0] * s.shape[2]
    n = s.shape[1] * 128
    return pl.pallas_call(
        solve_kernel,
        out_shape=(
            jax.ShapeDtypeStruct((k, n), F32),
            jax.ShapeDtypeStruct((k, k), F32),
        ),
        in_specs=[VMEM, VMEM],
        out_specs=(VMEM, VMEM),
        scratch_shapes=[pltpu.VMEM((k, k + n), F32)],
        compiler_params=PARAMS,
        name="orthonormalize",
    )(near(g), near(s))


def sum_over_devices(tiles):
    shape = tiles.shape
    rows = lax.axis_size("row")
    bundles = lax.axis_size("bundle")
    parts = lax.all_to_all(
        tiles.reshape(rows, -1, 128), "row", split_axis=0, concat_axis=0, tiled=True
    )
    mine = jnp.sum(parts, axis=0)
    parts = lax.all_to_all(
        jnp.broadcast_to(mine[None], (bundles,) + mine.shape),
        "bundle",
        split_axis=0,
        concat_axis=0,
        tiled=True,
    )
    mine = jnp.sum(parts, axis=0)
    parts = lax.all_to_all(
        jnp.broadcast_to(mine[None], (rows,) + mine.shape),
        "row",
        split_axis=0,
        concat_axis=0,
        tiled=True,
    )
    return parts.reshape(shape)


def local(vectors, blocks, columns, bounds):
    block_rows = blocks.shape[0]
    row_count = lax.axis_size("row")
    bundles = lax.axis_size("bundle")
    total_rows = block_rows * row_count
    first_row = lax.axis_index("row") * block_rows
    places = slot_places(columns, first_row, block_rows, total_rows)
    forward = [(i, (i + 1) % row_count) for i in range(row_count)]
    backward = [(j, i) for i, j in forward]

    def sides(field):
        return (
            lax.ppermute(field, "row", forward),
            lax.ppermute(field, "row", backward),
        )

    low, high = sides(vectors)
    w = split_blocks(blocks)
    first = apply_step(
        0, places, bounds, vectors, low, high, None, w
    )
    low, high = sides(first)
    second = apply_step(
        1, places, bounds, first, low, high, vectors, w
    )
    low, high = sides(second)
    filtered = apply_step(
        2, places, bounds, second, low, high, first, w
    )
    tiles, width, lanes = filtered.shape
    stacked = lax.all_to_all(
        filtered.reshape(bundles, tiles // bundles, width, lanes),
        "bundle",
        split_axis=0,
        concat_axis=0,
        tiled=True,
    )
    gram = sum_over_devices(gram_tiles(stacked))
    return orthonormalize(gram, stacked)


def solution(mesh):
    placed = (P("bundle", "row"), P("row", None, None), P("row", None), P())
    return jax.shard_map(
        local,
        mesh=mesh,
        in_specs=placed,
        out_specs=(P(None, ("row", "bundle")), P()),
        check_vma=False,
    )
```

```python
import functools

import jax
import jax.numpy as jnp
from jax import lax
from jax.experimental import pallas as pl
from jax.experimental.pallas import tpu as pltpu
from jax.sharding import PartitionSpec as P

BF = jnp.bfloat16
F32 = jnp.float32
HIGHEST = lax.Precision.HIGHEST
VMEM = pl.BlockSpec(memory_space=pltpu.VMEM)
SMEM = pl.BlockSpec(memory_space=pltpu.SMEM)
NB = 64
PACKED = 320
PLANE = 64
BUILD_UNROLL = 8
PAIR_UNROLL = 8
PARAMS = pltpu.CompilerParams(vmem_limit_bytes=20 * 1024 * 1024)


def near(x):
    return pltpu.with_memory_space_constraint(x, pltpu.VMEM)


def split(x):
    hi = x.astype(BF)
    lo = (x - hi.astype(F32)).astype(BF)
    return hi, lo


def dot_nt(a, b):
    return lax.dot_general(a, b, (((1,), (1,)), ((), ())), preferred_element_type=F32)


def split_kernel(b_ref, w_ref):
    hi, lo = split(b_ref[...])
    w_ref[:, 0:64, :] = hi
    w_ref[:, 64:128, :] = lo


def split_blocks(blocks):
    n, a, m = blocks.shape
    step = 8
    return pl.pallas_call(
        split_kernel,
        out_shape=pltpu.VMEM((n, 2 * a, m), BF),
        grid=(n // step,),
        in_specs=[pl.BlockSpec((step, a, m), lambda i: (i, 0, 0))],
        out_specs=pl.BlockSpec((step, 2 * a, m), lambda i: (i, 0, 0)),
        compiler_params=PARAMS,
        name="split_blocks",
    )(blocks)


def apply_kernel(stage, slot_ref, bounds_ref, *refs):
    if stage == 0:
        f_ref, low_ref, high_ref, w_ref, out_ref, e_ref = refs
        prev_ref = None
    else:
        f_ref, low_ref, high_ref, prev_ref, w_ref, out_ref, e_ref = refs
    width = f_ref.shape[0]
    tiles = f_ref.shape[1] // 128
    left = lax.broadcasted_iota(jnp.int32, (width, 128), 1) < 64
    left2 = lax.broadcasted_iota(jnp.int32, (2 * width, 128), 1) < 64

    def build(t, carry):
        for part, ref in enumerate((low_ref, f_ref, high_ref)):
            x = ref[:, pl.ds(pl.multiple_of(t * 128, 128), 128)]
            for v, y in enumerate((x, pltpu.roll(x, 64, 1))):
                hi, lo = split(y)
                at = (3 * v + part) * tiles + t
                e_ref[at, 0:width] = hi
                e_ref[at, width : 2 * width] = lo
        return carry

    lax.fori_loop(0, tiles, build, 0, unroll=BUILD_UNROLL)

    center = (bounds_ref[0] + bounds_ref[1]) * 0.5
    half = (bounds_ref[1] - bounds_ref[0]) * 0.5
    slots = w_ref.shape[2] // 64

    def one(i):
        at = [slot_ref[i * slots + s] for s in range(slots)]
        lhs = jnp.concatenate(
            [
                jnp.where(left2, e_ref[at[s]], e_ref[at[s + 1]])
                for s in range(0, slots, 2)
            ],
            axis=1,
        )
        out = dot_nt(lhs, w_ref[i])
        acc = out[:width] + jnp.where(left, out[width:], 0.0)
        return acc + pltpu.roll(acc, 64, 1)

    def pair(g, carry):
        y = jnp.where(left, one(2 * g), one(2 * g + 1))
        lanes = pl.ds(pl.multiple_of(g * 128, 128), 128)
        f = f_ref[:, lanes]
        r = (y - center * f) / half
        if stage > 0:
            r = 2.0 * r - prev_ref[:, lanes]
        if stage < 2:
            out_ref[:, lanes] = r
        else:
            out_ref[g] = r
        return carry

    lax.fori_loop(0, tiles, pair, 0, unroll=PAIR_UNROLL)


def apply_step(stage, slot_table, bounds, f, low, high, prev, w):
    width, n = f.shape
    tiles = n // 128
    args = (f, low, high) + (() if prev is None else (prev,)) + (w,)
    out = (width, n) if stage < 2 else (tiles, width, 128)
    return pl.pallas_call(
        functools.partial(apply_kernel, stage),
        out_shape=pltpu.VMEM(out, F32),
        in_specs=[SMEM] * 2 + [VMEM] * len(args),
        out_specs=VMEM,
        scratch_shapes=[pltpu.VMEM((6 * tiles, 2 * width, 128), BF)],
        compiler_params=PARAMS,
        name=f"apply_{stage}",
    )(slot_table, bounds, *map(near, args))


def slot_places(columns, first_row, block_rows, total_rows):
    reach = jnp.mod(columns - first_row + block_rows, total_rows)
    right = jnp.arange(columns.shape[1], dtype=jnp.int32) % 2
    exchanged = (reach + right) % 2
    return (exchanged * (3 * block_rows // 2) + reach // 2).reshape(-1)


def square():
    return (
        lax.broadcasted_iota(jnp.int32, (128, 128), 0),
        lax.broadcasted_iota(jnp.int32, (128, 128), 1),
    )


def gram_kernel(s_ref, out_ref):
    s = jnp.concatenate(
        [
            s_ref[:, j].reshape(s_ref.shape[0] * s_ref.shape[2], 128)
            for j in range(s_ref.shape[1])
        ],
        axis=1,
    )
    g = lax.dot_general(
        s, s, (((1,), (1,)), ((), ())), precision=HIGHEST, preferred_element_type=F32
    )
    row, col = square()
    last = g[128:, 128:]
    out_ref[0:128] = g[:128, 128:]
    out_ref[128:256] = jnp.where(row >= col, g[:128, :128], last)
    out_ref[256:] = jnp.zeros((out_ref.shape[0] - 256, 128), F32)
    out_ref[256:257] = jnp.sum(
        jnp.where(row == col, last, 0.0), axis=0, keepdims=True
    )


def gram_packed(s):
    return pl.pallas_call(
        gram_kernel,
        out_shape=pltpu.VMEM((PACKED, 128), F32),
        in_specs=[VMEM],
        out_specs=VMEM,
        compiler_params=PARAMS,
        name="gram",
    )(near(s))


def row_of(x, r):
    return jnp.take_along_axis(x, jnp.full((8, 128), r, jnp.int32), axis=0)


def lane_of(x, c):
    return jnp.broadcast_to(x[:, c : c + 1], (8, 128))


def factor_block(m):
    n = m.shape[0]
    sub = lax.broadcasted_iota(jnp.int32, (8, 128), 0)
    here = [sub == k for k in range(8)]
    vregs = [m[8 * v : 8 * v + 8] for v in range(n // 8)]
    done = []
    for v0 in range(n // 8):
        head = vregs[v0]
        cols = [
            [lane_of(vregs[v], 8 * v0 + c) for c in range(8)]
            for v in range(v0, n // 8)
        ]
        p = list(cols[0])
        out = jnp.zeros((8, 128), F32)
        for k in range(8):
            pivot = row_of(p[k], k)
            inv = 1.0 / pivot
            row = row_of(head, k)
            out = jnp.where(here[k], row * lax.rsqrt(pivot), out)
            for c in range(k + 1, 8):
                r = row_of(p[c], k) * inv
                p[c] = jnp.where(here[k], r, p[c] - p[k] * r)
            r = row * inv
            head = jnp.where(here[k], r, head - p[k] * r)
        done.append(out)
        if v0 + 1 == n // 8:
            break
        z = [row_of(head, k) for k in range(8)]
        for v in range(v0 + 1, n // 8):
            t = [cols[v - v0][k] * z[k] for k in range(8)]
            while len(t) > 1:
                t = [t[i] + t[i + 1] for i in range(0, len(t), 2)]
            vregs[v] = vregs[v] - t[0]
    return jnp.concatenate(done, axis=0)


def split3(x):
    a = x.astype(BF)
    r = x - a.astype(F32)
    b = r.astype(BF)
    c = (r - b.astype(F32)).astype(BF)
    return a, b, c


def six_lanes(twice):
    a, b, c = split3(twice)
    left = lax.broadcasted_iota(jnp.int32, twice.shape, 1) < NB
    return jnp.concatenate([a, jnp.where(left, b, a), jnp.where(left, b, c)], axis=1)


def six_rows(x):
    a, b, c = split3(x)
    return jnp.concatenate([a, b, a, c, b, a], axis=0)


def dot_nn(a, b):
    return lax.dot_general(a, b, (((1,), (0,)), ((), ())), preferred_element_type=F32)


def solve_kernel(g_ref, s_ref, basis_ref, factor_ref, a_ref):
    k = factor_ref.shape[0]
    row, col = square()
    mixed = g_ref[128:256]
    turned = mixed.T
    a_ref[:128, :128] = jnp.where(row >= col, mixed, turned)
    a_ref[:128, 128:k] = g_ref[0:128]
    last = jnp.where(row < col, mixed, turned)
    a_ref[128:, 128:k] = jnp.where(row == col, g_ref[256:257], last)
    for j in range(s_ref.shape[1]):
        a_ref[:, k + j * 128 : k + (j + 1) * 128] = s_ref[:, j].reshape(k, 128)
    lane = lax.broadcasted_iota(jnp.int32, (NB, 128), 1)
    sub = lax.broadcasted_iota(jnp.int32, (NB, 128), 0)
    eye = jnp.where(lane == sub + NB, 1.0, 0.0)
    for first in range(0, k, NB):
        rows = slice(first, first + NB)
        at = first // 128 * 128
        tile = a_ref[rows, at : at + 128]
        if first > at:
            tile = pltpu.roll(tile, NB, 1)
        u = factor_block(jnp.where(lane < NB, tile, eye))
        twice = jnp.where(lane < NB, pltpu.roll(u, NB, 1), u)
        x = dot_nn(six_lanes(twice), six_rows(a_ref[rows, at:]))
        col_id = at + lax.broadcasted_iota(jnp.int32, (NB, k - at), 1)
        row_id = first + lax.broadcasted_iota(jnp.int32, (NB, k - at), 0)
        upper = jnp.where(col_id >= row_id, x[:, : k - at], 0.0)
        if at > 0:
            upper = jnp.concatenate([jnp.zeros((NB, at), F32), upper], axis=1)
        factor_ref[rows, :] = upper
        basis_ref[rows, :] = x[:, k - at :]
        after = first + NB
        if after < k:
            start = after // 128 * 128
            turned = x[:, start - at : k - at]
            turned = jnp.concatenate([turned, turned], axis=0).T[after - start :]
            a_ref[after:, start:] -= dot_nn(
                six_lanes(turned), six_rows(x[:, start - at :])
            )


def orthonormalize(g, s):
    k = s.shape[0] * s.shape[2]
    n = s.shape[1] * 128
    return pl.pallas_call(
        solve_kernel,
        out_shape=(
            jax.ShapeDtypeStruct((k, n), F32),
            jax.ShapeDtypeStruct((k, k), F32),
        ),
        in_specs=[VMEM, VMEM],
        out_specs=(VMEM, VMEM),
        scratch_shapes=[pltpu.VMEM((k, k + n), F32)],
        compiler_params=PARAMS,
        name="orthonormalize",
    )(near(g), near(s))


def sum_over_devices(packed):
    axes = ("row", "bundle")
    count = lax.axis_size("row") * lax.axis_size("bundle")
    planes = count // PLANE
    plane = [[p * PLANE + i for i in range(PLANE)] for p in range(planes)]
    across = [[p * PLANE + i for p in range(planes)] for i in range(PLANE)]

    def exchange(x, groups):
        return lax.all_to_all(
            x, axes, 0, 0, axis_index_groups=groups, tiled=True
        )

    def copies(x, n):
        return jnp.broadcast_to(x[None], (n,) + x.shape)

    mine = jnp.sum(exchange(packed.reshape(PLANE, 1, -1), plane), axis=0)
    mine = jnp.sum(exchange(copies(mine, planes), across), axis=0)
    return exchange(copies(mine, PLANE), plane).reshape(packed.shape)


def local(vectors, blocks, columns, bounds):
    block_rows = blocks.shape[0]
    row_count = lax.axis_size("row")
    bundles = lax.axis_size("bundle")
    total_rows = block_rows * row_count
    first_row = lax.axis_index("row") * block_rows
    places = slot_places(columns, first_row, block_rows, total_rows)
    forward = [(i, (i + 1) % row_count) for i in range(row_count)]
    backward = [(j, i) for i, j in forward]

    def sides(field):
        return (
            lax.ppermute(field, "row", forward),
            lax.ppermute(field, "row", backward),
        )

    low, high = sides(vectors)
    w = split_blocks(blocks)
    first = apply_step(
        0, places, bounds, vectors, low, high, None, w
    )
    low, high = sides(first)
    second = apply_step(
        1, places, bounds, first, low, high, vectors, w
    )
    low, high = sides(second)
    filtered = apply_step(
        2, places, bounds, second, low, high, first, w
    )
    tiles, width, lanes = filtered.shape
    stacked = lax.all_to_all(
        filtered.reshape(bundles, tiles // bundles, width, lanes),
        "bundle",
        split_axis=0,
        concat_axis=0,
        tiled=True,
    )
    gram = sum_over_devices(gram_packed(stacked))
    return orthonormalize(gram, stacked)


def solution(mesh):
    placed = (P("bundle", "row"), P("row", None, None), P("row", None), P())
    return jax.shard_map(
        local,
        mesh=mesh,
        in_specs=placed,
        out_specs=(P(None, ("row", "bundle")), P()),
        check_vma=False,
    )
```

```python
import functools

import jax
import jax.numpy as jnp
from jax import lax
from jax.experimental import pallas as pl
from jax.experimental.pallas import tpu as pltpu
from jax.sharding import PartitionSpec as P

BF = jnp.bfloat16
F32 = jnp.float32
HIGHEST = lax.Precision.HIGHEST
VMEM = pl.BlockSpec(memory_space=pltpu.VMEM)
SMEM = pl.BlockSpec(memory_space=pltpu.SMEM)
NB = 64
PACKED = 320
BUILD_UNROLL = 8
PAIR_UNROLL = 8
PARAMS = pltpu.CompilerParams(vmem_limit_bytes=20 * 1024 * 1024)


def near(x):
    return pltpu.with_memory_space_constraint(x, pltpu.VMEM)


def split(x):
    hi = x.astype(BF)
    lo = (x - hi.astype(F32)).astype(BF)
    return hi, lo


def dot_nt(a, b):
    return lax.dot_general(a, b, (((1,), (1,)), ((), ())), preferred_element_type=F32)


def split_kernel(b_ref, w_ref):
    hi, lo = split(b_ref[...])
    w_ref[:, 0:64, :] = hi
    w_ref[:, 64:128, :] = lo


def split_blocks(blocks):
    n, a, m = blocks.shape
    step = 8
    return pl.pallas_call(
        split_kernel,
        out_shape=pltpu.VMEM((n, 2 * a, m), BF),
        grid=(n // step,),
        in_specs=[pl.BlockSpec((step, a, m), lambda i: (i, 0, 0))],
        out_specs=pl.BlockSpec((step, 2 * a, m), lambda i: (i, 0, 0)),
        compiler_params=PARAMS,
        name="split_blocks",
    )(blocks)


def apply_kernel(stage, slot_ref, bounds_ref, *refs):
    if stage == 0:
        f_ref, inner_ref, outer_ref, w_ref, out_ref, e_ref = refs
        prev_ref = None
    else:
        f_ref, inner_ref, outer_ref, prev_ref, w_ref, out_ref, e_ref = refs
    width = f_ref.shape[0]
    tiles = f_ref.shape[1] // 128
    left = lax.broadcasted_iota(jnp.int32, (width, 128), 1) < 64
    left2 = lax.broadcasted_iota(jnp.int32, (2 * width, 128), 1) < 64

    def build(t, carry):
        for part, ref in enumerate((inner_ref, f_ref, outer_ref)):
            x = ref[:, pl.ds(pl.multiple_of(t * 128, 128), 128)]
            for v, y in enumerate((x, pltpu.roll(x, 64, 1))):
                hi, lo = split(y)
                at = (3 * v + part) * tiles + t
                e_ref[at, 0:width] = hi
                e_ref[at, width : 2 * width] = lo
        return carry

    lax.fori_loop(0, tiles, build, 0, unroll=BUILD_UNROLL)

    center = (bounds_ref[0] + bounds_ref[1]) * 0.5
    half = (bounds_ref[1] - bounds_ref[0]) * 0.5
    slots = w_ref.shape[2] // 64

    def one(i):
        at = [slot_ref[i * slots + s] for s in range(slots)]
        lhs = jnp.concatenate(
            [
                jnp.where(left2, e_ref[at[s]], e_ref[at[s + 1]])
                for s in range(0, slots, 2)
            ],
            axis=1,
        )
        out = dot_nt(lhs, w_ref[i])
        acc = out[:width] + jnp.where(left, out[width:], 0.0)
        return acc + pltpu.roll(acc, 64, 1)

    def pair(g, carry):
        y = jnp.where(left, one(2 * g), one(2 * g + 1))
        lanes = pl.ds(pl.multiple_of(g * 128, 128), 128)
        f = f_ref[:, lanes]
        r = (y - center * f) / half
        if stage > 0:
            r = 2.0 * r - prev_ref[:, lanes]
        if stage < 2:
            out_ref[:, lanes] = r
        else:
            out_ref[g] = r
        return carry

    lax.fori_loop(0, tiles, pair, 0, unroll=PAIR_UNROLL)


def apply_step(stage, slot_table, bounds, f, inner, outer, prev, w):
    width, n = f.shape
    tiles = n // 128
    args = (f, inner, outer) + (() if prev is None else (prev,)) + (w,)
    out = (width, n) if stage < 2 else (tiles, width, 128)
    return pl.pallas_call(
        functools.partial(apply_kernel, stage),
        out_shape=pltpu.VMEM(out, F32),
        in_specs=[SMEM] * 2 + [VMEM] * len(args),
        out_specs=VMEM,
        scratch_shapes=[pltpu.VMEM((6 * tiles, 2 * width, 128), BF)],
        compiler_params=PARAMS,
        name=f"apply_{stage}",
    )(slot_table, bounds, *map(near, args))


def slot_places(columns, row, block_rows, total_rows):
    reach = jnp.mod(columns - (row - 1) * block_rows, total_rows)
    side, inner = reach // block_rows, reach % block_rows
    side = jnp.where(row % 2 == 0, 2 - side, side)
    right = jnp.arange(columns.shape[1], dtype=jnp.int32) % 2
    exchanged = (inner + right) % 2
    tiles = block_rows // 2
    return ((exchanged * 3 + side) * tiles + inner // 2).reshape(-1)


def square():
    return (
        lax.broadcasted_iota(jnp.int32, (128, 128), 0),
        lax.broadcasted_iota(jnp.int32, (128, 128), 1),
    )


def gram_kernel(s_ref, out_ref):
    s = jnp.concatenate(
        [
            s_ref[:, j].reshape(s_ref.shape[0] * s_ref.shape[2], 128)
            for j in range(s_ref.shape[1])
        ],
        axis=1,
    )
    g = lax.dot_general(
        s, s, (((1,), (1,)), ((), ())), precision=HIGHEST, preferred_element_type=F32
    )
    row, col = square()
    last = g[128:, 128:]
    out_ref[0:128] = g[:128, 128:]
    out_ref[128:256] = jnp.where(row >= col, g[:128, :128], last)
    out_ref[256:] = jnp.zeros((out_ref.shape[0] - 256, 128), F32)
    out_ref[256:257] = jnp.sum(
        jnp.where(row == col, last, 0.0), axis=0, keepdims=True
    )


def gram_packed(s):
    return pl.pallas_call(
        gram_kernel,
        out_shape=pltpu.VMEM((PACKED, 128), F32),
        in_specs=[VMEM],
        out_specs=VMEM,
        compiler_params=PARAMS,
        name="gram",
    )(near(s))


def row_of(x, r):
    return jnp.take_along_axis(x, jnp.full((8, 128), r, jnp.int32), axis=0)


def lane_of(x, c):
    return jnp.broadcast_to(x[:, c : c + 1], (8, 128))


def factor_block(m):
    n = m.shape[0]
    sub = lax.broadcasted_iota(jnp.int32, (8, 128), 0)
    here = [sub == k for k in range(8)]
    vregs = [m[8 * v : 8 * v + 8] for v in range(n // 8)]
    done = []
    for v0 in range(n // 8):
        head = vregs[v0]
        cols = [
            [lane_of(vregs[v], 8 * v0 + c) for c in range(8)]
            for v in range(v0, n // 8)
        ]
        p = list(cols[0])
        out = jnp.zeros((8, 128), F32)
        for k in range(8):
            pivot = row_of(p[k], k)
            inv = 1.0 / pivot
            row = row_of(head, k)
            out = jnp.where(here[k], row * lax.rsqrt(pivot), out)
            for c in range(k + 1, 8):
                r = row_of(p[c], k) * inv
                p[c] = jnp.where(here[k], r, p[c] - p[k] * r)
            r = row * inv
            head = jnp.where(here[k], r, head - p[k] * r)
        done.append(out)
        if v0 + 1 == n // 8:
            break
        z = [row_of(head, k) for k in range(8)]
        for v in range(v0 + 1, n // 8):
            t = [cols[v - v0][k] * z[k] for k in range(8)]
            while len(t) > 1:
                t = [t[i] + t[i + 1] for i in range(0, len(t), 2)]
            vregs[v] = vregs[v] - t[0]
    return jnp.concatenate(done, axis=0)


def split3(x):
    a = x.astype(BF)
    r = x - a.astype(F32)
    b = r.astype(BF)
    c = (r - b.astype(F32)).astype(BF)
    return a, b, c


def six_lanes(twice):
    a, b, c = split3(twice)
    left = lax.broadcasted_iota(jnp.int32, twice.shape, 1) < NB
    return jnp.concatenate([a, jnp.where(left, b, a), jnp.where(left, b, c)], axis=1)


def six_rows(x):
    a, b, c = split3(x)
    return jnp.concatenate([a, b, a, c, b, a], axis=0)


def dot_nn(a, b):
    return lax.dot_general(a, b, (((1,), (0,)), ((), ())), preferred_element_type=F32)


def solve_kernel(g_ref, s_ref, basis_ref, factor_ref, a_ref):
    k = factor_ref.shape[0]
    row, col = square()
    mixed = g_ref[128:256]
    turned = mixed.T
    a_ref[:128, :128] = jnp.where(row >= col, mixed, turned)
    a_ref[:128, 128:k] = g_ref[0:128]
    last = jnp.where(row < col, mixed, turned)
    a_ref[128:, 128:k] = jnp.where(row == col, g_ref[256:257], last)
    for j in range(s_ref.shape[1]):
        a_ref[:, k + j * 128 : k + (j + 1) * 128] = s_ref[:, j].reshape(k, 128)
    lane = lax.broadcasted_iota(jnp.int32, (NB, 128), 1)
    sub = lax.broadcasted_iota(jnp.int32, (NB, 128), 0)
    eye = jnp.where(lane == sub + NB, 1.0, 0.0)
    for first in range(0, k, NB):
        rows = slice(first, first + NB)
        at = first // 128 * 128
        tile = a_ref[rows, at : at + 128]
        if first > at:
            tile = pltpu.roll(tile, NB, 1)
        u = factor_block(jnp.where(lane < NB, tile, eye))
        twice = jnp.where(lane < NB, pltpu.roll(u, NB, 1), u)
        x = dot_nn(six_lanes(twice), six_rows(a_ref[rows, at:]))
        col_id = at + lax.broadcasted_iota(jnp.int32, (NB, k - at), 1)
        row_id = first + lax.broadcasted_iota(jnp.int32, (NB, k - at), 0)
        upper = jnp.where(col_id >= row_id, x[:, : k - at], 0.0)
        if at > 0:
            upper = jnp.concatenate([jnp.zeros((NB, at), F32), upper], axis=1)
        factor_ref[rows, :] = upper
        basis_ref[rows, :] = x[:, k - at :]
        after = first + NB
        if after < k:
            start = after // 128 * 128
            turned = x[:, start - at : k - at]
            turned = jnp.concatenate([turned, turned], axis=0).T[after - start :]
            a_ref[after:, start:] -= dot_nn(
                six_lanes(turned), six_rows(x[:, start - at :])
            )


def orthonormalize(g, s):
    k = s.shape[0] * s.shape[2]
    n = s.shape[1] * 128
    return pl.pallas_call(
        solve_kernel,
        out_shape=(
            jax.ShapeDtypeStruct((k, n), F32),
            jax.ShapeDtypeStruct((k, k), F32),
        ),
        in_specs=[VMEM, VMEM],
        out_specs=(VMEM, VMEM),
        scratch_shapes=[pltpu.VMEM((k, k + n), F32)],
        compiler_params=PARAMS,
        name="orthonormalize",
    )(near(g), near(s))


def sum_over_devices(packed):
    axes = ("row", "bundle")
    rows, bundles = lax.axis_size("row"), lax.axis_size("bundle")
    chips, planes = bundles // 2, 8
    line = rows // planes
    part = chips * line

    def device(z, y, x, core):
        return ((z * line + y) * chips + x) * 2 + core

    plane = [
        [device(z, y, x, core) for y in range(line) for x in range(chips)]
        for z in range(planes)
        for core in range(2)
    ]
    across = [
        [device(z, y, x, core) for z in range(planes) for core in range(2)]
        for y in range(line)
        for x in range(chips)
    ]

    def exchange(x, groups):
        return lax.all_to_all(
            x, axes, 0, 0, axis_index_groups=groups, tiled=True
        )

    def copies(x, n):
        return jnp.broadcast_to(x[None], (n,) + x.shape)

    mine = jnp.sum(exchange(packed.reshape(part, 1, -1), plane), axis=0)
    mine = jnp.sum(exchange(copies(mine, 2 * planes), across), axis=0)
    return exchange(copies(mine, part), plane).reshape(packed.shape)


def local(vectors, blocks, columns, bounds):
    block_rows = blocks.shape[0]
    row_count = lax.axis_size("row")
    bundles = lax.axis_size("bundle")
    total_rows = block_rows * row_count
    places = slot_places(
        columns, lax.axis_index("row"), block_rows, total_rows
    )
    inside = [(i, i ^ 1) for i in range(row_count)]
    outside = [
        (i, (i + 1 if i % 2 else i - 1) % row_count) for i in range(row_count)
    ]

    def sides(field):
        return (
            lax.ppermute(field, "row", inside),
            lax.ppermute(field, "row", outside),
        )

    inner, outer = sides(vectors)
    w = split_blocks(blocks)
    first = apply_step(
        0, places, bounds, vectors, inner, outer, None, w
    )
    inner, outer = sides(first)
    second = apply_step(
        1, places, bounds, first, inner, outer, vectors, w
    )
    inner, outer = sides(second)
    filtered = apply_step(
        2, places, bounds, second, inner, outer, first, w
    )
    tiles, width, lanes = filtered.shape
    stacked = lax.all_to_all(
        filtered.reshape(bundles, tiles // bundles, width, lanes),
        "bundle",
        split_axis=0,
        concat_axis=0,
        tiled=True,
    )
    gram = sum_over_devices(gram_packed(stacked))
    return orthonormalize(gram, stacked)


def solution(mesh):
    placed = (P("bundle", "row"), P("row", None, None), P("row", None), P())
    return jax.shard_map(
        local,
        mesh=mesh,
        in_specs=placed,
        out_specs=(P(None, ("row", "bundle")), P()),
        check_vma=False,
    )
```

```python
import functools

import jax
import jax.numpy as jnp
from jax import lax
from jax.experimental import pallas as pl
from jax.experimental.pallas import tpu as pltpu
from jax.sharding import PartitionSpec as P

BF = jnp.bfloat16
F32 = jnp.float32
HIGHEST = lax.Precision.HIGHEST
VMEM = pl.BlockSpec(memory_space=pltpu.VMEM)
SMEM = pl.BlockSpec(memory_space=pltpu.SMEM)
NB = 64
PACKED = 320
BUILD_UNROLL = 8
PAIR_UNROLL = 8
PARAMS = pltpu.CompilerParams(vmem_limit_bytes=20 * 1024 * 1024)


def near(x):
    return pltpu.with_memory_space_constraint(x, pltpu.VMEM)


def split(x):
    hi = x.astype(BF)
    lo = (x - hi.astype(F32)).astype(BF)
    return hi, lo


def dot_nt(a, b):
    return lax.dot_general(a, b, (((1,), (1,)), ((), ())), preferred_element_type=F32)


def split_kernel(b_ref, w_ref):
    for i in range(b_ref.shape[0]):
        hi, lo = split(b_ref[i])
        both = jnp.concatenate([hi.astype(F32), lo.astype(F32)], axis=0)
        w_ref[i] = both.T.astype(BF)


def split_blocks(blocks):
    n, a, m = blocks.shape
    step = 8
    return pl.pallas_call(
        split_kernel,
        out_shape=pltpu.VMEM((n, m, 2 * a), BF),
        grid=(n // step,),
        in_specs=[pl.BlockSpec((step, a, m), lambda i: (i, 0, 0))],
        out_specs=pl.BlockSpec((step, m, 2 * a), lambda i: (i, 0, 0)),
        compiler_params=PARAMS,
        name="split_blocks",
    )(blocks)


def apply_kernel(stage, slot_ref, bounds_ref, *refs):
    if stage == 0:
        f_ref, inner_ref, outer_ref, w_ref, out_ref, e_ref = refs
        prev_ref = None
    else:
        f_ref, inner_ref, outer_ref, prev_ref, w_ref, out_ref, e_ref = refs
    width = f_ref.shape[0]
    tiles = f_ref.shape[1] // 128
    left = lax.broadcasted_iota(jnp.int32, (width, 128), 1) < 64
    left2 = lax.broadcasted_iota(jnp.int32, (2 * width, 128), 1) < 64

    def build(t, carry):
        for part, ref in enumerate((inner_ref, f_ref, outer_ref)):
            x = ref[:, pl.ds(pl.multiple_of(t * 128, 128), 128)]
            for v, y in enumerate((x, pltpu.roll(x, 64, 1))):
                hi, lo = split(y)
                at = (3 * v + part) * tiles + t
                e_ref[at, 0:width] = hi
                e_ref[at, width : 2 * width] = lo
        return carry

    lax.fori_loop(0, tiles, build, 0, unroll=BUILD_UNROLL)

    center = (bounds_ref[0] + bounds_ref[1]) * 0.5
    half = (bounds_ref[1] - bounds_ref[0]) * 0.5
    slots = w_ref.shape[1] // 64

    def one(i):
        at = [slot_ref[i * slots + s] for s in range(slots)]
        lhs = jnp.concatenate(
            [
                jnp.where(left2, e_ref[at[s]], e_ref[at[s + 1]])
                for s in range(0, slots, 2)
            ],
            axis=1,
        )
        out = dot_nn(lhs, w_ref[i])
        acc = out[:width] + jnp.where(left, out[width:], 0.0)
        return acc + pltpu.roll(acc, 64, 1)

    def pair(g, carry):
        y = jnp.where(left, one(2 * g), one(2 * g + 1))
        lanes = pl.ds(pl.multiple_of(g * 128, 128), 128)
        f = f_ref[:, lanes]
        r = (y - center * f) / half
        if stage > 0:
            r = 2.0 * r - prev_ref[:, lanes]
        if stage < 2:
            out_ref[:, lanes] = r
        else:
            out_ref[g] = r
        return carry

    lax.fori_loop(0, tiles, pair, 0, unroll=PAIR_UNROLL)


def apply_step(stage, slot_table, bounds, f, inner, outer, prev, w):
    width, n = f.shape
    tiles = n // 128
    args = (f, inner, outer) + (() if prev is None else (prev,)) + (w,)
    out = (width, n) if stage < 2 else (tiles, width, 128)
    return pl.pallas_call(
        functools.partial(apply_kernel, stage),
        out_shape=pltpu.VMEM(out, F32),
        in_specs=[SMEM] * 2 + [VMEM] * len(args),
        out_specs=VMEM,
        scratch_shapes=[pltpu.VMEM((6 * tiles, 2 * width, 128), BF)],
        compiler_params=PARAMS,
        name=f"apply_{stage}",
    )(slot_table, bounds, *map(near, args))


def slot_places(columns, row, block_rows, total_rows):
    reach = jnp.mod(columns - (row - 1) * block_rows, total_rows)
    side, inner = reach // block_rows, reach % block_rows
    side = jnp.where(row % 2 == 0, 2 - side, side)
    right = jnp.arange(columns.shape[1], dtype=jnp.int32) % 2
    exchanged = (inner + right) % 2
    tiles = block_rows // 2
    return ((exchanged * 3 + side) * tiles + inner // 2).reshape(-1)


def square():
    return (
        lax.broadcasted_iota(jnp.int32, (128, 128), 0),
        lax.broadcasted_iota(jnp.int32, (128, 128), 1),
    )


def gram_kernel(s_ref, out_ref):
    s = jnp.concatenate(
        [
            s_ref[:, j].reshape(s_ref.shape[0] * s_ref.shape[2], 128)
            for j in range(s_ref.shape[1])
        ],
        axis=1,
    )
    g = lax.dot_general(
        s, s, (((1,), (1,)), ((), ())), precision=HIGHEST, preferred_element_type=F32
    )
    row, col = square()
    last = g[128:, 128:]
    out_ref[0:128] = g[:128, 128:]
    out_ref[128:256] = jnp.where(row >= col, g[:128, :128], last)
    out_ref[256:] = jnp.zeros((out_ref.shape[0] - 256, 128), F32)
    out_ref[256:257] = jnp.sum(
        jnp.where(row == col, last, 0.0), axis=0, keepdims=True
    )


def gram_packed(s):
    return pl.pallas_call(
        gram_kernel,
        out_shape=pltpu.VMEM((PACKED, 128), F32),
        in_specs=[VMEM],
        out_specs=VMEM,
        compiler_params=PARAMS,
        name="gram",
    )(near(s))


def row_of(x, r):
    return jnp.take_along_axis(x, jnp.full((8, 128), r, jnp.int32), axis=0)


def lane_of(x, c):
    return jnp.broadcast_to(x[:, c : c + 1], (8, 128))


def factor_block(m):
    n = m.shape[0]
    sub = lax.broadcasted_iota(jnp.int32, (8, 128), 0)
    here = [sub == k for k in range(8)]
    vregs = [m[8 * v : 8 * v + 8] for v in range(n // 8)]
    done = []

    def update(some, v0, z):
        sums = {}
        for k in range(8):
            for v in some:
                t = lane_of(vregs[v], 8 * v0 + k) * z[k]
                sums[v] = sums[v] + t if k else t
        for v in some:
            vregs[v] = vregs[v] - sums[v]

    for v0 in range(n // 8):
        head = vregs[v0]
        p = [lane_of(head, 8 * v0 + c) for c in range(8)]
        out = jnp.zeros((8, 128), F32)
        for k in range(0, 8, 2):
            a, b, d = row_of(p[k], k), row_of(p[k + 1], k), row_of(p[k + 1], k + 1)
            det = a * d - b * b
            inv = 1.0 / det

            def eliminate(x):
                s0, s1 = row_of(x, k), row_of(x, k + 1)
                w0, w1 = d * s0 - b * s1, a * s1 - b * s0
                y = x - (p[k] * w0 + p[k + 1] * w1) * inv
                y = jnp.where(here[k], w0 * inv, y)
                return jnp.where(here[k + 1], w1 * inv, y), s0, w1

            for c in range(k + 2, 8):
                p[c] = eliminate(p[c])[0]
            head, s0, w1 = eliminate(head)
            out = jnp.where(here[k], s0 * lax.rsqrt(a), out)
            out = jnp.where(here[k + 1], w1 * lax.rsqrt(a * det), out)
        done.append(out)
        z = [row_of(head, k) for k in range(8)]
        for some in ([v0 + 1], list(range(v0 + 2, n // 8))):
            if some and some[0] < n // 8:
                update(some, v0, z)
    return jnp.concatenate(done, axis=0)


def split3(x):
    a = x.astype(BF)
    r = x - a.astype(F32)
    b = r.astype(BF)
    c = (r - b.astype(F32)).astype(BF)
    return a, b, c


def six_lanes(twice):
    a, b, c = split3(twice)
    left = lax.broadcasted_iota(jnp.int32, twice.shape, 1) < NB
    return jnp.concatenate([a, jnp.where(left, b, a), jnp.where(left, b, c)], axis=1)


def six_rows(x):
    a, b, c = split3(x)
    return jnp.concatenate([a, b, a, c, b, a], axis=0)


def dot_nn(a, b):
    return lax.dot_general(a, b, (((1,), (0,)), ((), ())), preferred_element_type=F32)


def solve_kernel(g_ref, s_ref, basis_ref, factor_ref, a_ref):
    k = factor_ref.shape[0]
    row, col = square()
    mixed = g_ref[128:256]
    turned = mixed.T
    diag = [
        jnp.sum(jnp.where(row == col, mixed, 0.0), axis=0, keepdims=True),
        g_ref[256:257],
    ]
    right = [jnp.broadcast_to(lax.rsqrt(d), (128, 128)) for d in diag]
    left = [r.T for r in right]
    size = [jnp.sqrt(d) for d in diag]
    a_ref[:128, :128] = jnp.where(row >= col, mixed, turned) * left[0] * right[0]
    a_ref[:128, 128:k] = g_ref[0:128] * left[0] * right[1]
    last = jnp.where(row < col, mixed, turned)
    last = jnp.where(row == col, diag[1], last)
    a_ref[128:, 128:k] = last * left[1] * right[1]
    for j in range(s_ref.shape[1]):
        at = k + j * 128
        part = s_ref[:, j].reshape(k, 128)
        a_ref[:128, at : at + 128] = part[:128] * left[0]
        a_ref[128:, at : at + 128] = part[128:] * left[1]
    size = jnp.concatenate(size, axis=1)
    lane = lax.broadcasted_iota(jnp.int32, (NB, 128), 1)
    sub = lax.broadcasted_iota(jnp.int32, (NB, 128), 0)
    eye = jnp.where(lane == sub + NB, 1.0, 0.0)
    for first in range(0, k, NB):
        rows = slice(first, first + NB)
        at = first // 128 * 128
        tile = a_ref[rows, at : at + 128]
        if first > at:
            tile = pltpu.roll(tile, NB, 1)
        u = factor_block(jnp.where(lane < NB, tile, eye))
        twice = jnp.where(lane < NB, pltpu.roll(u, NB, 1), u)
        x = dot_nn(six_lanes(twice), six_rows(a_ref[rows, at:]))
        col_id = at + lax.broadcasted_iota(jnp.int32, (NB, k - at), 1)
        row_id = first + lax.broadcasted_iota(jnp.int32, (NB, k - at), 0)
        upper = jnp.where(col_id >= row_id, x[:, : k - at] * size[:, at:], 0.0)
        if at > 0:
            upper = jnp.concatenate([jnp.zeros((NB, at), F32), upper], axis=1)
        factor_ref[rows, :] = upper
        basis_ref[rows, :] = x[:, k - at :]
        after = first + NB
        if after < k:
            start = after // 128 * 128
            turned = x[:, start - at : k - at]
            turned = jnp.concatenate([turned, turned], axis=0).T[after - start :]
            a_ref[after:, start:] -= dot_nn(
                six_lanes(turned), six_rows(x[:, start - at :])
            )


def orthonormalize(g, s):
    k = s.shape[0] * s.shape[2]
    n = s.shape[1] * 128
    return pl.pallas_call(
        solve_kernel,
        out_shape=(
            jax.ShapeDtypeStruct((k, n), F32),
            jax.ShapeDtypeStruct((k, k), F32),
        ),
        in_specs=[VMEM, VMEM],
        out_specs=(VMEM, VMEM),
        scratch_shapes=[pltpu.VMEM((k, k + n), F32)],
        compiler_params=PARAMS,
        name="orthonormalize",
    )(near(g), near(s))


def sum_over_devices(packed):
    axes = ("row", "bundle")
    rows, bundles = lax.axis_size("row"), lax.axis_size("bundle")
    chips, planes = bundles // 2, 8
    line = rows // planes
    part = chips * line

    def device(z, y, x, core):
        return ((z * line + y) * chips + x) * 2 + core

    plane = [
        [device(z, y, x, core) for y in range(line) for x in range(chips)]
        for z in range(planes)
        for core in range(2)
    ]
    across = [
        [device(z, y, x, core) for z in range(planes) for core in range(2)]
        for y in range(line)
        for x in range(chips)
    ]

    def exchange(x, groups):
        return lax.all_to_all(
            x, axes, 0, 0, axis_index_groups=groups, tiled=True
        )

    def copies(x, n):
        return jnp.broadcast_to(x[None], (n,) + x.shape)

    mine = jnp.sum(exchange(packed.reshape(part, 1, -1), plane), axis=0)
    mine = jnp.sum(exchange(copies(mine, 2 * planes), across), axis=0)
    return exchange(copies(mine, part), plane).reshape(packed.shape)


def local(vectors, blocks, columns, bounds):
    block_rows = blocks.shape[0]
    row_count = lax.axis_size("row")
    bundles = lax.axis_size("bundle")
    total_rows = block_rows * row_count
    places = slot_places(
        columns, lax.axis_index("row"), block_rows, total_rows
    )
    inside = [(i, i ^ 1) for i in range(row_count)]
    outside = [
        (i, (i + 1 if i % 2 else i - 1) % row_count) for i in range(row_count)
    ]

    def sides(field):
        return (
            lax.ppermute(field, "row", inside),
            lax.ppermute(field, "row", outside),
        )

    inner, outer = sides(vectors)
    w = split_blocks(blocks)
    first = apply_step(
        0, places, bounds, vectors, inner, outer, None, w
    )
    inner, outer = sides(first)
    second = apply_step(
        1, places, bounds, first, inner, outer, vectors, w
    )
    inner, outer = sides(second)
    filtered = apply_step(
        2, places, bounds, second, inner, outer, first, w
    )
    tiles, width, lanes = filtered.shape
    stacked = lax.all_to_all(
        filtered.reshape(bundles, tiles // bundles, width, lanes),
        "bundle",
        split_axis=0,
        concat_axis=0,
        tiled=True,
    )
    gram = sum_over_devices(gram_packed(stacked))
    return orthonormalize(gram, stacked)


def solution(mesh):
    placed = (P("bundle", "row"), P("row", None, None), P("row", None), P())
    return jax.shard_map(
        local,
        mesh=mesh,
        in_specs=placed,
        out_specs=(P(None, ("row", "bundle")), P()),
        check_vma=False,
    )
```

```python
import functools

import jax
import jax.numpy as jnp
from jax import lax
from jax.experimental import pallas as pl
from jax.experimental.pallas import tpu as pltpu
from jax.sharding import PartitionSpec as P

BF = jnp.bfloat16
F32 = jnp.float32
HIGHEST = lax.Precision.HIGHEST
VMEM = pl.BlockSpec(memory_space=pltpu.VMEM)
SMEM = pl.BlockSpec(memory_space=pltpu.SMEM)
NB = 64
PACKED = 320
BUILD_UNROLL = 8
AHEAD = 8
PAIR_UNROLL = 8
PARAMS = pltpu.CompilerParams(vmem_limit_bytes=20 * 1024 * 1024)


def near(x):
    return pltpu.with_memory_space_constraint(x, pltpu.VMEM)


def split(x):
    hi = x.astype(BF)
    lo = (x - hi.astype(F32)).astype(BF)
    return hi, lo


def dot_nt(a, b):
    return lax.dot_general(a, b, (((1,), (1,)), ((), ())), preferred_element_type=F32)


def split_kernel(b_ref, w_ref):
    for i in range(b_ref.shape[0]):
        hi, lo = split(b_ref[i])
        both = jnp.concatenate([hi.astype(F32), lo.astype(F32)], axis=0)
        w_ref[i] = both.T.astype(BF)


def split_blocks(blocks):
    n, a, m = blocks.shape
    step = 8
    return pl.pallas_call(
        split_kernel,
        out_shape=pltpu.VMEM((n, m, 2 * a), BF),
        grid=(n // step,),
        in_specs=[pl.BlockSpec((step, a, m), lambda i: (i, 0, 0))],
        out_specs=pl.BlockSpec((step, m, 2 * a), lambda i: (i, 0, 0)),
        compiler_params=PARAMS,
        name="split_blocks",
    )(blocks)


def apply_kernel(stage, slot_ref, bounds_ref, *refs):
    if stage == 0:
        f_ref, inner_ref, outer_ref, w_ref, out_ref, e_ref = refs
        prev_ref = None
    else:
        f_ref, inner_ref, outer_ref, prev_ref, w_ref, out_ref, e_ref = refs
    width = f_ref.shape[0]
    tiles = f_ref.shape[1] // 128
    left = lax.broadcasted_iota(jnp.int32, (width, 128), 1) < 64
    left2 = lax.broadcasted_iota(jnp.int32, (2 * width, 128), 1) < 64

    def build(t, carry):
        for part, ref in enumerate((inner_ref, f_ref, outer_ref)):
            x = ref[:, pl.ds(pl.multiple_of(t * 128, 128), 128)]
            for v, y in enumerate((x, pltpu.roll(x, 64, 1))):
                hi, lo = split(y)
                at = (3 * v + part) * tiles + t
                e_ref[at, 0:width] = hi
                e_ref[at, width : 2 * width] = lo
        return carry

    lax.fori_loop(0, tiles, build, 0, unroll=BUILD_UNROLL)

    center = (bounds_ref[0] + bounds_ref[1]) * 0.5
    half = (bounds_ref[1] - bounds_ref[0]) * 0.5
    slots = w_ref.shape[1] // 64

    def one(i):
        at = [slot_ref[i * slots + s] for s in range(slots)]
        lhs = jnp.concatenate(
            [
                jnp.where(left2, e_ref[at[s]], e_ref[at[s + 1]])
                for s in range(0, slots, 2)
            ],
            axis=1,
        )
        out = dot_nn(lhs, w_ref[i])
        acc = out[:width] + jnp.where(left, out[width:], 0.0)
        return acc + pltpu.roll(acc, 64, 1)

    def pair(g, carry):
        y = jnp.where(left, one(2 * g), one(2 * g + 1))
        lanes = pl.ds(pl.multiple_of(g * 128, 128), 128)
        f = f_ref[:, lanes]
        r = (y - center * f) / half
        if stage > 0:
            r = 2.0 * r - prev_ref[:, lanes]
        if stage < 2:
            out_ref[:, lanes] = r
        else:
            out_ref[g] = r
        return carry

    lax.fori_loop(0, tiles, pair, 0, unroll=PAIR_UNROLL)


def apply_step(stage, slot_table, bounds, f, inner, outer, prev, w):
    width, n = f.shape
    tiles = n // 128
    args = (f, inner, outer) + (() if prev is None else (prev,)) + (w,)
    out = (width, n) if stage < 2 else (tiles, width, 128)
    return pl.pallas_call(
        functools.partial(apply_kernel, stage),
        out_shape=pltpu.VMEM(out, F32),
        in_specs=[SMEM] * 2 + [VMEM] * len(args),
        out_specs=VMEM,
        scratch_shapes=[pltpu.VMEM((6 * tiles, 2 * width, 128), BF)],
        compiler_params=PARAMS,
        name=f"apply_{stage}",
    )(slot_table, bounds, *map(near, args))


def slot_places(columns, row, block_rows, total_rows):
    reach = jnp.mod(columns - (row - 1) * block_rows, total_rows)
    side, inner = reach // block_rows, reach % block_rows
    side = jnp.where(row % 2 == 0, 2 - side, side)
    right = jnp.arange(columns.shape[1], dtype=jnp.int32) % 2
    exchanged = (inner + right) % 2
    tiles = block_rows // 2
    return ((exchanged * 3 + side) * tiles + inner // 2).reshape(-1)


def square():
    return (
        lax.broadcasted_iota(jnp.int32, (128, 128), 0),
        lax.broadcasted_iota(jnp.int32, (128, 128), 1),
    )


def gram_kernel(s_ref, out_ref):
    s = jnp.concatenate(
        [
            s_ref[:, j].reshape(s_ref.shape[0] * s_ref.shape[2], 128)
            for j in range(s_ref.shape[1])
        ],
        axis=1,
    )
    g = lax.dot_general(
        s, s, (((1,), (1,)), ((), ())), precision=HIGHEST, preferred_element_type=F32
    )
    row, col = square()
    last = g[128:, 128:]
    out_ref[0:128] = g[:128, 128:]
    out_ref[128:256] = jnp.where(row >= col, g[:128, :128], last)
    out_ref[256:] = jnp.zeros((out_ref.shape[0] - 256, 128), F32)
    out_ref[256:257] = jnp.sum(
        jnp.where(row == col, last, 0.0), axis=0, keepdims=True
    )


def gram_packed(s):
    return pl.pallas_call(
        gram_kernel,
        out_shape=pltpu.VMEM((PACKED, 128), F32),
        in_specs=[VMEM],
        out_specs=VMEM,
        compiler_params=PARAMS,
        name="gram",
    )(near(s))


def row_of(x, r):
    return jnp.take_along_axis(x, jnp.full((8, 128), r, jnp.int32), axis=0)


def lane_of(x, c):
    return jnp.broadcast_to(x[:, c : c + 1], (8, 128))


def factor_block(m):
    n = m.shape[0]
    sub = lax.broadcasted_iota(jnp.int32, (8, 128), 0)
    here = [sub == k for k in range(8)]
    vregs = [m[8 * v : 8 * v + 8] for v in range(n // 8)]
    done = []

    def update(some, v0, z):
        sums = {}
        for k in range(8):
            for v in some:
                t = lane_of(vregs[v], 8 * v0 + k) * z[k]
                sums[v] = sums[v] + t if k else t
        for v in some:
            vregs[v] = vregs[v] - sums[v]

    early = []
    for v0 in range(n // 8):
        head = vregs[v0]
        p = early + [lane_of(head, 8 * v0 + c) for c in range(len(early), 8)]
        more = AHEAD if v0 + 1 < n // 8 else 0
        p += [lane_of(head, 8 * v0 + 8 + c) for c in range(more)]
        out = jnp.zeros((8, 128), F32)
        for k in range(0, 8, 2):
            a, b, d = row_of(p[k], k), row_of(p[k + 1], k), row_of(p[k + 1], k + 1)
            det = a * d - b * b
            inv = 1.0 / det

            both = here[k] | here[k + 1]
            m0 = jnp.where(both, jnp.where(here[k], -1.0, 0.0), p[k])
            m1 = jnp.where(both, jnp.where(here[k + 1], -1.0, 0.0), p[k + 1])

            def eliminate(x):
                s0, s1 = row_of(x, k), row_of(x, k + 1)
                w0, w1 = d * s0 - b * s1, a * s1 - b * s0
                y = jnp.where(both, 0.0, x) - (m0 * w0 + m1 * w1) * inv
                return y, s0, w1

            for c in range(k + 2, 8 + more):
                p[c] = eliminate(p[c])[0]
            head, s0, w1 = eliminate(head)
            out = jnp.where(here[k], s0 * lax.rsqrt(a), out)
            out = jnp.where(here[k + 1], w1 * lax.rsqrt(a * det), out)
        done.append(out)
        early = []
        for c in range(more):
            t = [
                lane_of(vregs[v0 + 1], 8 * v0 + k) * row_of(p[8 + c], k)
                for k in range(8)
            ]
            while len(t) > 1:
                t = [t[i] + t[i + 1] for i in range(0, len(t), 2)]
            early.append(lane_of(vregs[v0 + 1], 8 * v0 + 8 + c) - t[0])
        z = [row_of(head, k) for k in range(8)]
        for some in ([v0 + 1], list(range(v0 + 2, n // 8))):
            if some and some[0] < n // 8:
                update(some, v0, z)
    return jnp.concatenate(done, axis=0)


def split3(x):
    a = x.astype(BF)
    r = x - a.astype(F32)
    b = r.astype(BF)
    c = (r - b.astype(F32)).astype(BF)
    return a, b, c


def six_lanes(twice):
    a, b, c = split3(twice)
    left = lax.broadcasted_iota(jnp.int32, twice.shape, 1) < NB
    return jnp.concatenate([a, jnp.where(left, b, a), jnp.where(left, b, c)], axis=1)


def six_rows(x):
    a, b, c = split3(x)
    return jnp.concatenate([a, b, a, c, b, a], axis=0)


def dot_nn(a, b):
    return lax.dot_general(a, b, (((1,), (0,)), ((), ())), preferred_element_type=F32)


def solve_kernel(
    g_ref, s_ref, basis_out, factor_out, a_ref, basis_ref, factor_ref, sems
):
    k = factor_ref.shape[0]
    copies = []
    row, col = square()
    mixed = g_ref[128:256]
    turned = mixed.T
    diag = [
        jnp.sum(jnp.where(row == col, mixed, 0.0), axis=0, keepdims=True),
        g_ref[256:257],
    ]
    right = [jnp.broadcast_to(lax.rsqrt(d), (128, 128)) for d in diag]
    left = [r.T for r in right]
    size = [jnp.sqrt(d) for d in diag]
    a_ref[:128, :128] = jnp.where(row >= col, mixed, turned) * left[0] * right[0]
    a_ref[:128, 128:k] = g_ref[0:128] * left[0] * right[1]
    last = jnp.where(row < col, mixed, turned)
    last = jnp.where(row == col, diag[1], last)
    a_ref[128:, 128:k] = last * left[1] * right[1]
    for j in range(s_ref.shape[1]):
        at = k + j * 128
        part = s_ref[:, j].reshape(k, 128)
        a_ref[:128, at : at + 128] = part[:128] * left[0]
        a_ref[128:, at : at + 128] = part[128:] * left[1]
    size = jnp.concatenate(size, axis=1)
    lane = lax.broadcasted_iota(jnp.int32, (NB, 128), 1)
    sub = lax.broadcasted_iota(jnp.int32, (NB, 128), 0)
    eye = jnp.where(lane == sub + NB, 1.0, 0.0)
    def rest(first, twice):
        rows, at, after = slice(first, first + NB), first // 128 * 128, first + NB
        x = dot_nn(six_lanes(twice), six_rows(a_ref[rows, at:]))
        col_id = at + lax.broadcasted_iota(jnp.int32, (NB, k - at), 1)
        row_id = first + lax.broadcasted_iota(jnp.int32, (NB, k - at), 0)
        upper = jnp.where(col_id >= row_id, x[:, : k - at] * size[:, at:], 0.0)
        if at > 0:
            upper = jnp.concatenate([jnp.zeros((NB, at), F32), upper], axis=1)
        factor_ref[rows, :] = upper
        basis_ref[rows, :] = x[:, k - at :]
        for i, (src, dst) in enumerate(
            ((basis_ref, basis_out), (factor_ref, factor_out))
        ):
            copy = pltpu.make_async_copy(
                src.at[rows, :], dst.at[rows, :], sems.at[i, first // NB]
            )
            copy.start()
            copies.append(copy)
        if after == k:
            return
        start = after // 128 * 128
        right = six_rows(x[:, start - at :])
        turned = x[:, start - at : k - at]
        turned = jnp.concatenate([turned, turned], axis=0).T[after - start :]
        left = six_lanes(turned)
        a_ref[after : after + NB, start + 128 :] -= dot_nn(left[:NB], right[:, 128:])
        if after + NB < k:
            a_ref[after + NB :, start:] -= dot_nn(left[NB:], right)

    def ahead(first, twice):
        rows, after = slice(first, first + NB), first + NB
        start = after // 128 * 128
        x = dot_nn(six_lanes(twice), six_rows(a_ref[rows, start : start + 128]))
        turned = jnp.concatenate([x, x], axis=0).T
        turned = turned[after - start : after - start + NB]
        return a_ref[after : after + NB, start : start + 128] - dot_nn(
            six_lanes(turned), six_rows(x)
        )

    for first in range(0, k, NB):
        at = first // 128 * 128
        if first == 0:
            tile = a_ref[0:NB, 0:128]
        elif first > at:
            tile = pltpu.roll(tile, NB, 1)
        u = factor_block(jnp.where(lane < NB, tile, eye))
        twice = jnp.where(lane < NB, pltpu.roll(u, NB, 1), u)
        if first + NB < k:
            tile = ahead(first, twice)
            rest(first, twice)
            nxt = first + NB
            a_ref[nxt : nxt + NB, nxt // 128 * 128 : nxt // 128 * 128 + 128] = tile
    rest(k - NB, twice)
    for copy in copies:
        copy.wait()


def orthonormalize(g, s):
    k = s.shape[0] * s.shape[2]
    n = s.shape[1] * 128
    return pl.pallas_call(
        solve_kernel,
        out_shape=(
            jax.ShapeDtypeStruct((k, n), F32),
            jax.ShapeDtypeStruct((k, k), F32),
        ),
        in_specs=[VMEM, VMEM],
        out_specs=(pl.BlockSpec(memory_space=pl.ANY),) * 2,
        scratch_shapes=[
            pltpu.VMEM((k, k + n), F32),
            pltpu.VMEM((k, n), F32),
            pltpu.VMEM((k, k), F32),
            pltpu.SemaphoreType.DMA((2, k // NB)),
        ],
        compiler_params=PARAMS,
        name="orthonormalize",
    )(near(g), near(s))


def sum_over_devices(packed):
    axes = ("row", "bundle")
    rows, bundles = lax.axis_size("row"), lax.axis_size("bundle")
    chips, planes = bundles // 2, 8
    line = rows // planes
    part = chips * line

    def device(z, y, x, core):
        return ((z * line + y) * chips + x) * 2 + core

    plane = [
        [device(z, y, x, core) for y in range(line) for x in range(chips)]
        for z in range(planes)
        for core in range(2)
    ]
    across = [
        [device(z, y, x, core) for z in range(planes) for core in range(2)]
        for y in range(line)
        for x in range(chips)
    ]

    def exchange(x, groups):
        return lax.all_to_all(
            x, axes, 0, 0, axis_index_groups=groups, tiled=True
        )

    def copies(x, n):
        return jnp.broadcast_to(x[None], (n,) + x.shape)

    mine = jnp.sum(exchange(packed.reshape(part, 1, -1), plane), axis=0)
    mine = jnp.sum(exchange(copies(mine, 2 * planes), across), axis=0)
    return exchange(copies(mine, part), plane).reshape(packed.shape)


def local(vectors, blocks, columns, bounds):
    block_rows = blocks.shape[0]
    row_count = lax.axis_size("row")
    bundles = lax.axis_size("bundle")
    total_rows = block_rows * row_count
    places = slot_places(
        columns, lax.axis_index("row"), block_rows, total_rows
    )
    inside = [(i, i ^ 1) for i in range(row_count)]
    outside = [
        (i, (i + 1 if i % 2 else i - 1) % row_count) for i in range(row_count)
    ]

    def sides(field):
        return (
            lax.ppermute(field, "row", inside),
            lax.ppermute(field, "row", outside),
        )

    inner, outer = sides(vectors)
    w = split_blocks(blocks)
    first = apply_step(
        0, places, bounds, vectors, inner, outer, None, w
    )
    inner, outer = sides(first)
    second = apply_step(
        1, places, bounds, first, inner, outer, vectors, w
    )
    inner, outer = sides(second)
    filtered = apply_step(
        2, places, bounds, second, inner, outer, first, w
    )
    tiles, width, lanes = filtered.shape
    stacked = lax.all_to_all(
        filtered.reshape(bundles, tiles // bundles, width, lanes),
        "bundle",
        split_axis=0,
        concat_axis=0,
        tiled=True,
    )
    gram = sum_over_devices(gram_packed(stacked))
    return orthonormalize(gram, stacked)


def solution(mesh):
    placed = (P("bundle", "row"), P("row", None, None), P("row", None), P())
    return jax.shard_map(
        local,
        mesh=mesh,
        in_specs=placed,
        out_specs=(P(None, ("row", "bundle")), P()),
        check_vma=False,
    )
```

```python
import functools

import jax
import jax.numpy as jnp
from jax import lax
from jax.experimental import pallas as pl
from jax.experimental.pallas import tpu as pltpu
from jax.sharding import PartitionSpec as P

BF = jnp.bfloat16
F32 = jnp.float32
HIGHEST = lax.Precision.HIGHEST
VMEM = pl.BlockSpec(memory_space=pltpu.VMEM)
SMEM = pl.BlockSpec(memory_space=pltpu.SMEM)
NB = 64
PACKED = 320
AHEAD = 8
PARAMS = pltpu.CompilerParams(vmem_limit_bytes=20 * 1024 * 1024)


def near(x):
    return pltpu.with_memory_space_constraint(x, pltpu.VMEM)


def split(x):
    hi = x.astype(BF)
    lo = (x - hi.astype(F32)).astype(BF)
    return hi, lo


def dot_nt(a, b):
    return lax.dot_general(a, b, (((1,), (1,)), ((), ())), preferred_element_type=F32)


def split_kernel(b_ref, w_ref):
    for i in range(b_ref.shape[0]):
        hi, lo = split(b_ref[i])
        both = jnp.concatenate([hi.astype(F32), lo.astype(F32)], axis=0)
        w_ref[i] = both.T.astype(BF)


def split_blocks(blocks):
    n, a, m = blocks.shape
    step = 8
    return pl.pallas_call(
        split_kernel,
        out_shape=pltpu.VMEM((n, m, 2 * a), BF),
        grid=(n // step,),
        in_specs=[pl.BlockSpec((step, a, m), lambda i: (i, 0, 0))],
        out_specs=pl.BlockSpec((step, m, 2 * a), lambda i: (i, 0, 0)),
        compiler_params=PARAMS,
        name="split_blocks",
    )(blocks)


def apply_kernel(stage, slot_ref, bounds_ref, *refs):
    if stage == 0:
        f_ref, inner_ref, outer_ref, w_ref, out_ref, e_ref = refs
        prev_ref = None
    else:
        f_ref, inner_ref, outer_ref, prev_ref, w_ref, out_ref, e_ref = refs
    width = f_ref.shape[0]
    tiles = f_ref.shape[1] // 128
    left = lax.broadcasted_iota(jnp.int32, (width, 128), 1) < 64
    left2 = lax.broadcasted_iota(jnp.int32, (2 * width, 128), 1) < 64

    def build(t):
        for part, ref in enumerate((inner_ref, f_ref, outer_ref)):
            x = ref[:, t * 128 : (t + 1) * 128]
            for v, y in enumerate((x, pltpu.roll(x, 64, 1))):
                hi, lo = split(y)
                at = (3 * v + part) * tiles + t
                e_ref[at, 0:width] = hi
                e_ref[at, width : 2 * width] = lo

    for t in range(tiles):
        build(t)

    center = (bounds_ref[0] + bounds_ref[1]) * 0.5
    half = (bounds_ref[1] - bounds_ref[0]) * 0.5
    slots = w_ref.shape[1] // 64

    def one(i):
        at = [slot_ref[i * slots + s] for s in range(slots)]
        lhs = jnp.concatenate(
            [
                jnp.where(left2, e_ref[at[s]], e_ref[at[s + 1]])
                for s in range(0, slots, 2)
            ],
            axis=1,
        )
        out = dot_nn(lhs, w_ref[i])
        acc = out[:width] + jnp.where(left, out[width:], 0.0)
        return acc + pltpu.roll(acc, 64, 1)

    def pair(g):
        y = jnp.where(left, one(2 * g), one(2 * g + 1))
        lanes = slice(g * 128, (g + 1) * 128)
        f = f_ref[:, lanes]
        r = (y - center * f) / half
        if stage > 0:
            r = 2.0 * r - prev_ref[:, lanes]
        if stage < 2:
            out_ref[:, lanes] = r
        else:
            out_ref[g] = r

    for g in range(tiles):
        pair(g)


def apply_step(stage, slot_table, bounds, f, inner, outer, prev, w):
    width, n = f.shape
    tiles = n // 128
    args = (f, inner, outer) + (() if prev is None else (prev,)) + (w,)
    out = (width, n) if stage < 2 else (tiles, width, 128)
    return pl.pallas_call(
        functools.partial(apply_kernel, stage),
        out_shape=pltpu.VMEM(out, F32),
        in_specs=[SMEM] * 2 + [VMEM] * len(args),
        out_specs=VMEM,
        scratch_shapes=[pltpu.VMEM((6 * tiles, 2 * width, 128), BF)],
        compiler_params=PARAMS,
        name=f"apply_{stage}",
    )(slot_table, bounds, *map(near, args))


def slot_places(columns, row, block_rows, total_rows):
    reach = jnp.mod(columns - (row - 1) * block_rows, total_rows)
    side, inner = reach // block_rows, reach % block_rows
    side = jnp.where(row % 2 == 0, 2 - side, side)
    right = jnp.arange(columns.shape[1], dtype=jnp.int32) % 2
    exchanged = (inner + right) % 2
    tiles = block_rows // 2
    return ((exchanged * 3 + side) * tiles + inner // 2).reshape(-1)


def square():
    return (
        lax.broadcasted_iota(jnp.int32, (128, 128), 0),
        lax.broadcasted_iota(jnp.int32, (128, 128), 1),
    )


def gram_kernel(s_ref, out_ref):
    s = jnp.concatenate(
        [
            s_ref[:, j].reshape(s_ref.shape[0] * s_ref.shape[2], 128)
            for j in range(s_ref.shape[1])
        ],
        axis=1,
    )
    g = lax.dot_general(
        s, s, (((1,), (1,)), ((), ())), precision=HIGHEST, preferred_element_type=F32
    )
    row, col = square()
    last = g[128:, 128:]
    out_ref[0:128] = g[:128, 128:]
    out_ref[128:256] = jnp.where(row >= col, g[:128, :128], last)
    out_ref[256:] = jnp.zeros((out_ref.shape[0] - 256, 128), F32)
    out_ref[256:257] = jnp.sum(
        jnp.where(row == col, last, 0.0), axis=0, keepdims=True
    )


def gram_packed(s):
    return pl.pallas_call(
        gram_kernel,
        out_shape=pltpu.VMEM((PACKED, 128), F32),
        in_specs=[VMEM],
        out_specs=VMEM,
        compiler_params=PARAMS,
        name="gram",
    )(near(s))


def row_of(x, r):
    return jnp.take_along_axis(x, jnp.full((8, 128), r, jnp.int32), axis=0)


def lane_of(x, c):
    return jnp.broadcast_to(x[:, c : c + 1], (8, 128))


def factor_block(m):
    n = m.shape[0]
    sub = lax.broadcasted_iota(jnp.int32, (8, 128), 0)
    here = [sub == k for k in range(8)]
    vregs = [m[8 * v : 8 * v + 8] for v in range(n // 8)]
    done = []

    def update(some, v0, z):
        sums = {}
        for k in range(8):
            for v in some:
                t = lane_of(vregs[v], 8 * v0 + k) * z[k]
                sums[v] = sums[v] + t if k else t
        for v in some:
            vregs[v] = vregs[v] - sums[v]

    early = []
    for v0 in range(n // 8):
        head = vregs[v0]
        p = early + [lane_of(head, 8 * v0 + c) for c in range(len(early), 8)]
        more = AHEAD if v0 + 1 < n // 8 else 0
        p += [lane_of(head, 8 * v0 + 8 + c) for c in range(more)]
        out = jnp.zeros((8, 128), F32)
        for k in range(0, 8, 2):
            a, b, d = row_of(p[k], k), row_of(p[k + 1], k), row_of(p[k + 1], k + 1)
            det = a * d - b * b
            inv = 1.0 / det

            both = here[k] | here[k + 1]
            m0 = jnp.where(both, jnp.where(here[k], -1.0, 0.0), p[k])
            m1 = jnp.where(both, jnp.where(here[k + 1], -1.0, 0.0), p[k + 1])

            def eliminate(x):
                s0, s1 = row_of(x, k), row_of(x, k + 1)
                w0, w1 = d * s0 - b * s1, a * s1 - b * s0
                y = jnp.where(both, 0.0, x) - (m0 * w0 + m1 * w1) * inv
                return y, s0, w1

            for c in range(k + 2, 8 + more):
                p[c] = eliminate(p[c])[0]
            head, s0, w1 = eliminate(head)
            out = jnp.where(here[k], s0 * lax.rsqrt(a), out)
            out = jnp.where(here[k + 1], w1 * lax.rsqrt(a * det), out)
        done.append(out)
        early = []
        for c in range(more):
            t = [
                lane_of(vregs[v0 + 1], 8 * v0 + k) * row_of(p[8 + c], k)
                for k in range(8)
            ]
            while len(t) > 1:
                t = [t[i] + t[i + 1] for i in range(0, len(t), 2)]
            early.append(lane_of(vregs[v0 + 1], 8 * v0 + 8 + c) - t[0])
        z = [row_of(head, k) for k in range(8)]
        for some in ([v0 + 1], list(range(v0 + 2, n // 8))):
            if some and some[0] < n // 8:
                update(some, v0, z)
    return jnp.concatenate(done, axis=0)


def split3(x):
    a = x.astype(BF)
    r = x - a.astype(F32)
    b = r.astype(BF)
    c = (r - b.astype(F32)).astype(BF)
    return a, b, c


def six_lanes(twice):
    a, b, c = split3(twice)
    left = lax.broadcasted_iota(jnp.int32, twice.shape, 1) < NB
    return jnp.concatenate([a, jnp.where(left, b, a), jnp.where(left, b, c)], axis=1)


def six_rows(x):
    a, b, c = split3(x)
    return jnp.concatenate([a, b, a, c, b, a], axis=0)


def dot_nn(a, b):
    return lax.dot_general(a, b, (((1,), (0,)), ((), ())), preferred_element_type=F32)


def solve_kernel(
    g_ref, s_ref, basis_out, factor_out, a_ref, basis_ref, factor_ref, sems
):
    k = factor_ref.shape[0]
    copies = []
    row, col = square()
    mixed = g_ref[128:256]
    turned = mixed.T
    diag = [
        jnp.sum(jnp.where(row == col, mixed, 0.0), axis=0, keepdims=True),
        g_ref[256:257],
    ]
    right = [jnp.broadcast_to(lax.rsqrt(d), (128, 128)) for d in diag]
    left = [r.T for r in right]
    size = [jnp.sqrt(d) for d in diag]
    a_ref[:128, :128] = jnp.where(row >= col, mixed, turned) * left[0] * right[0]
    a_ref[:128, 128:k] = g_ref[0:128] * left[0] * right[1]
    last = jnp.where(row < col, mixed, turned)
    last = jnp.where(row == col, diag[1], last)
    a_ref[128:, 128:k] = last * left[1] * right[1]
    for j in range(s_ref.shape[1]):
        at = k + j * 128
        part = s_ref[:, j].reshape(k, 128)
        a_ref[:128, at : at + 128] = part[:128] * left[0]
        a_ref[128:, at : at + 128] = part[128:] * left[1]
    size = jnp.concatenate(size, axis=1)
    lane = lax.broadcasted_iota(jnp.int32, (NB, 128), 1)
    sub = lax.broadcasted_iota(jnp.int32, (NB, 128), 0)
    eye = jnp.where(lane == sub + NB, 1.0, 0.0)
    def rest(first, twice):
        rows, at, after = slice(first, first + NB), first // 128 * 128, first + NB
        x = dot_nn(six_lanes(twice), six_rows(a_ref[rows, at:]))
        col_id = at + lax.broadcasted_iota(jnp.int32, (NB, k - at), 1)
        row_id = first + lax.broadcasted_iota(jnp.int32, (NB, k - at), 0)
        upper = jnp.where(col_id >= row_id, x[:, : k - at] * size[:, at:], 0.0)
        if at > 0:
            upper = jnp.concatenate([jnp.zeros((NB, at), F32), upper], axis=1)
        factor_ref[rows, :] = upper
        basis_ref[rows, :] = x[:, k - at :]
        for i, (src, dst) in enumerate(
            ((basis_ref, basis_out), (factor_ref, factor_out))
        ):
            copy = pltpu.make_async_copy(
                src.at[rows, :], dst.at[rows, :], sems.at[i, first // NB]
            )
            copy.start()
            copies.append(copy)
        if after == k:
            return
        start = after // 128 * 128
        right = six_rows(x[:, start - at :])
        turned = x[:, start - at : k - at]
        turned = jnp.concatenate([turned, turned], axis=0).T[after - start :]
        left = six_lanes(turned)
        a_ref[after : after + NB, start + 128 :] -= dot_nn(left[:NB], right[:, 128:])
        if after + NB < k:
            a_ref[after + NB :, start:] -= dot_nn(left[NB:], right)

    def ahead(first, twice):
        rows, after = slice(first, first + NB), first + NB
        start = after // 128 * 128
        x = dot_nn(six_lanes(twice), six_rows(a_ref[rows, start : start + 128]))
        turned = jnp.concatenate([x, x], axis=0).T
        turned = turned[after - start : after - start + NB]
        return a_ref[after : after + NB, start : start + 128] - dot_nn(
            six_lanes(turned), six_rows(x)
        )

    for first in range(0, k, NB):
        at = first // 128 * 128
        if first == 0:
            tile = a_ref[0:NB, 0:128]
        elif first > at:
            tile = pltpu.roll(tile, NB, 1)
        u = factor_block(jnp.where(lane < NB, tile, eye))
        twice = jnp.where(lane < NB, pltpu.roll(u, NB, 1), u)
        if first + NB < k:
            tile = ahead(first, twice)
            rest(first, twice)
            nxt = first + NB
            a_ref[nxt : nxt + NB, nxt // 128 * 128 : nxt // 128 * 128 + 128] = tile
    rest(k - NB, twice)
    for copy in copies:
        copy.wait()


def orthonormalize(g, s):
    k = s.shape[0] * s.shape[2]
    n = s.shape[1] * 128
    return pl.pallas_call(
        solve_kernel,
        out_shape=(
            jax.ShapeDtypeStruct((k, n), F32),
            jax.ShapeDtypeStruct((k, k), F32),
        ),
        in_specs=[VMEM, VMEM],
        out_specs=(pl.BlockSpec(memory_space=pl.ANY),) * 2,
        scratch_shapes=[
            pltpu.VMEM((k, k + n), F32),
            pltpu.VMEM((k, n), F32),
            pltpu.VMEM((k, k), F32),
            pltpu.SemaphoreType.DMA((2, k // NB)),
        ],
        compiler_params=PARAMS,
        name="orthonormalize",
    )(near(g), near(s))


def sum_over_devices(packed):
    axes = ("row", "bundle")
    rows, bundles = lax.axis_size("row"), lax.axis_size("bundle")
    chips, planes = bundles // 2, 8
    line = rows // planes
    part = chips * line

    def device(z, y, x, core):
        return ((z * line + y) * chips + x) * 2 + core

    plane = [
        [device(z, y, x, core) for y in range(line) for x in range(chips)]
        for z in range(planes)
        for core in range(2)
    ]
    across = [
        [device(z, y, x, core) for z in range(planes) for core in range(2)]
        for y in range(line)
        for x in range(chips)
    ]

    def exchange(x, groups):
        return lax.all_to_all(
            x, axes, 0, 0, axis_index_groups=groups, tiled=True
        )

    def copies(x, n):
        return jnp.broadcast_to(x[None], (n,) + x.shape)

    mine = jnp.sum(exchange(packed.reshape(part, 1, -1), plane), axis=0)
    mine = jnp.sum(exchange(copies(mine, 2 * planes), across), axis=0)
    return exchange(copies(mine, part), plane).reshape(packed.shape)


def local(vectors, blocks, columns, bounds):
    block_rows = blocks.shape[0]
    row_count = lax.axis_size("row")
    bundles = lax.axis_size("bundle")
    total_rows = block_rows * row_count
    places = slot_places(
        columns, lax.axis_index("row"), block_rows, total_rows
    )
    inside = [(i, i ^ 1) for i in range(row_count)]
    outside = [
        (i, (i + 1 if i % 2 else i - 1) % row_count) for i in range(row_count)
    ]

    def sides(field):
        return (
            lax.ppermute(field, "row", inside),
            lax.ppermute(field, "row", outside),
        )

    inner, outer = sides(vectors)
    w = split_blocks(blocks)
    first = apply_step(
        0, places, bounds, vectors, inner, outer, None, w
    )
    inner, outer = sides(first)
    second = apply_step(
        1, places, bounds, first, inner, outer, vectors, w
    )
    inner, outer = sides(second)
    filtered = apply_step(
        2, places, bounds, second, inner, outer, first, w
    )
    tiles, width, lanes = filtered.shape
    stacked = lax.all_to_all(
        filtered.reshape(bundles, tiles // bundles, width, lanes),
        "bundle",
        split_axis=0,
        concat_axis=0,
        tiled=True,
    )
    gram = sum_over_devices(gram_packed(stacked))
    return orthonormalize(gram, stacked)


def solution(mesh):
    placed = (P("bundle", "row"), P("row", None, None), P("row", None), P())
    return jax.shard_map(
        local,
        mesh=mesh,
        in_specs=placed,
        out_specs=(P(None, ("row", "bundle")), P()),
        check_vma=False,
    )
```

```python
import functools

import jax
import jax.numpy as jnp
from jax import lax
from jax.experimental import pallas as pl
from jax.experimental.pallas import tpu as pltpu
from jax.sharding import PartitionSpec as P

BF = jnp.bfloat16
F32 = jnp.float32
HIGHEST = lax.Precision.HIGHEST
VMEM = pl.BlockSpec(memory_space=pltpu.VMEM)
SMEM = pl.BlockSpec(memory_space=pltpu.SMEM)
NB = 64
PACKED = 320
AHEAD = 8
PARAMS = pltpu.CompilerParams(vmem_limit_bytes=20 * 1024 * 1024)


def near(x):
    return pltpu.with_memory_space_constraint(x, pltpu.VMEM)


def split(x):
    hi = x.astype(BF)
    lo = (x - hi.astype(F32)).astype(BF)
    return hi, lo


def dot_nt(a, b):
    return lax.dot_general(a, b, (((1,), (1,)), ((), ())), preferred_element_type=F32)


def split_kernel(b_ref, w_ref):
    for i in range(b_ref.shape[0]):
        hi, lo = split(b_ref[i])
        both = jnp.concatenate([hi.astype(F32), lo.astype(F32)], axis=0)
        w_ref[i] = both.T.astype(BF)


def split_blocks(blocks):
    n, a, m = blocks.shape
    step = 8
    return pl.pallas_call(
        split_kernel,
        out_shape=pltpu.VMEM((n, m, 2 * a), BF),
        grid=(n // step,),
        in_specs=[pl.BlockSpec((step, a, m), lambda i: (i, 0, 0))],
        out_specs=pl.BlockSpec((step, m, 2 * a), lambda i: (i, 0, 0)),
        compiler_params=PARAMS,
        name="split_blocks",
    )(blocks)


def apply_kernel(stage, slot_ref, bounds_ref, *refs):
    if stage == 0:
        f_ref, inner_ref, outer_ref, w_ref, out_ref, e_ref = refs
        prev_ref = None
    else:
        f_ref, inner_ref, outer_ref, prev_ref, w_ref, out_ref, e_ref = refs
    width = f_ref.shape[0]
    tiles = f_ref.shape[1] // 128
    left = lax.broadcasted_iota(jnp.int32, (width, 128), 1) < 64
    left2 = lax.broadcasted_iota(jnp.int32, (2 * width, 128), 1) < 64

    def build(t):
        for part, ref in enumerate((inner_ref, f_ref, outer_ref)):
            x = ref[:, t * 128 : (t + 1) * 128]
            for v, y in enumerate((x, pltpu.roll(x, 64, 1))):
                hi, lo = split(y)
                at = (3 * v + part) * tiles + t
                e_ref[at, 0:width] = hi
                e_ref[at, width : 2 * width] = lo

    for t in range(tiles):
        build(t)

    center = (bounds_ref[0] + bounds_ref[1]) * 0.5
    half = (bounds_ref[1] - bounds_ref[0]) * 0.5
    slots = w_ref.shape[1] // 64

    def one(i):
        at = [slot_ref[i * slots + s] for s in range(slots)]
        lhs = jnp.concatenate(
            [
                jnp.where(left2, e_ref[at[s]], e_ref[at[s + 1]])
                for s in range(0, slots, 2)
            ],
            axis=1,
        )
        out = dot_nn(lhs, w_ref[i])
        acc = out[:width] + jnp.where(left, out[width:], 0.0)
        return acc + pltpu.roll(acc, 64, 1)

    def pair(g):
        y = jnp.where(left, one(2 * g), one(2 * g + 1))
        lanes = slice(g * 128, (g + 1) * 128)
        f = f_ref[:, lanes]
        r = (y - center * f) / half
        if stage > 0:
            r = 2.0 * r - prev_ref[:, lanes]
        if stage < 2:
            out_ref[:, lanes] = r
        else:
            out_ref[g] = r

    for g in range(tiles):
        pair(g)


def apply_step(stage, slot_table, bounds, f, inner, outer, prev, w):
    width, n = f.shape
    tiles = n // 128
    args = (f, inner, outer) + (() if prev is None else (prev,)) + (w,)
    out = (width, n) if stage < 2 else (tiles, width, 128)
    return pl.pallas_call(
        functools.partial(apply_kernel, stage),
        out_shape=pltpu.VMEM(out, F32),
        in_specs=[SMEM] * 2 + [VMEM] * len(args),
        out_specs=VMEM,
        scratch_shapes=[pltpu.VMEM((6 * tiles, 2 * width, 128), BF)],
        compiler_params=PARAMS,
        name=f"apply_{stage}",
    )(slot_table, bounds, *map(near, args))


def slot_places(columns, row, block_rows, total_rows):
    reach = jnp.mod(columns - (row - 1) * block_rows, total_rows)
    side, inner = reach // block_rows, reach % block_rows
    side = jnp.where(row % 2 == 0, 2 - side, side)
    right = jnp.arange(columns.shape[1], dtype=jnp.int32) % 2
    exchanged = (inner + right) % 2
    tiles = block_rows // 2
    return ((exchanged * 3 + side) * tiles + inner // 2).reshape(-1)


def square():
    return (
        lax.broadcasted_iota(jnp.int32, (128, 128), 0),
        lax.broadcasted_iota(jnp.int32, (128, 128), 1),
    )


def gram_kernel(s_ref, out_ref):
    s = jnp.concatenate(
        [
            s_ref[:, j].reshape(s_ref.shape[0] * s_ref.shape[2], 128)
            for j in range(s_ref.shape[1])
        ],
        axis=1,
    )
    g = lax.dot_general(
        s, s, (((1,), (1,)), ((), ())), precision=HIGHEST, preferred_element_type=F32
    )
    row, col = square()
    last = g[128:, 128:]
    out_ref[0:128] = g[:128, 128:]
    out_ref[128:256] = jnp.where(row >= col, g[:128, :128], last)
    out_ref[256:] = jnp.zeros((out_ref.shape[0] - 256, 128), F32)
    out_ref[256:257] = jnp.sum(
        jnp.where(row == col, last, 0.0), axis=0, keepdims=True
    )


def gram_packed(s):
    return pl.pallas_call(
        gram_kernel,
        out_shape=pltpu.VMEM((PACKED, 128), F32),
        in_specs=[VMEM],
        out_specs=VMEM,
        compiler_params=PARAMS,
        name="gram",
    )(near(s))


def row_of(x, r):
    return jnp.take_along_axis(x, jnp.full((8, 128), r, jnp.int32), axis=0)


def lane_of(x, c):
    return jnp.broadcast_to(x[:, c : c + 1], (8, 128))


def factor_block(m, aside=()):
    aside = list(aside)
    n = m.shape[0]
    sub = lax.broadcasted_iota(jnp.int32, (8, 128), 0)
    here = [sub == k for k in range(8)]
    vregs = [m[8 * v : 8 * v + 8] for v in range(n // 8)]
    done = []

    def update(some, v0, z):
        sums = {}
        for k in range(8):
            for v in some:
                t = lane_of(vregs[v], 8 * v0 + k) * z[k]
                sums[v] = sums[v] + t if k else t
        for v in some:
            vregs[v] = vregs[v] - sums[v]

    early = []
    for v0 in range(n // 8):
        head = vregs[v0]
        p = early + [lane_of(head, 8 * v0 + c) for c in range(len(early), 8)]
        more = AHEAD if v0 + 1 < n // 8 else 0
        p += [lane_of(head, 8 * v0 + 8 + c) for c in range(more)]
        out = jnp.zeros((8, 128), F32)
        for k in range(0, 8, 2):
            a, b, d = row_of(p[k], k), row_of(p[k + 1], k), row_of(p[k + 1], k + 1)
            det = a * d - b * b
            inv = 1.0 / det

            both = here[k] | here[k + 1]
            m0 = jnp.where(both, jnp.where(here[k], -1.0, 0.0), p[k])
            m1 = jnp.where(both, jnp.where(here[k + 1], -1.0, 0.0), p[k + 1])

            n0, n1 = m0 * d - m1 * b, m1 * a - m0 * b

            def eliminate(x):
                s0, s1 = row_of(x, k), row_of(x, k + 1)
                return jnp.where(both, 0.0, x) - (s0 * n0 + s1 * n1) * inv

            for c in range(k + 2, 8 + more):
                p[c] = eliminate(p[c])
            s0 = row_of(head, k)
            w1 = a * row_of(head, k + 1) - b * s0
            head = eliminate(head)
            out = jnp.where(here[k], s0 * lax.rsqrt(a), out)
            out = jnp.where(here[k + 1], w1 * lax.rsqrt(a * det), out)
        done.append(out)
        for _ in range(-(-len(aside) // max(1, n // 8 - 1 - v0))):
            aside.pop(0)()
        early = []
        for c in range(more):
            t = [
                lane_of(vregs[v0 + 1], 8 * v0 + k) * row_of(p[8 + c], k)
                for k in range(8)
            ]
            while len(t) > 1:
                t = [t[i] + t[i + 1] for i in range(0, len(t), 2)]
            early.append(lane_of(vregs[v0 + 1], 8 * v0 + 8 + c) - t[0])
        z = [row_of(head, k) for k in range(8)]
        for some in ([v0 + 1], list(range(v0 + 2, n // 8))):
            if some and some[0] < n // 8:
                update(some, v0, z)
    return jnp.concatenate(done, axis=0)


def split3(x):
    a = x.astype(BF)
    r = x - a.astype(F32)
    b = r.astype(BF)
    c = (r - b.astype(F32)).astype(BF)
    return a, b, c


def six_lanes(twice):
    a, b, c = split3(twice)
    left = lax.broadcasted_iota(jnp.int32, twice.shape, 1) < NB
    return jnp.concatenate([a, jnp.where(left, b, a), jnp.where(left, b, c)], axis=1)


def six_rows(x):
    a, b, c = split3(x)
    return jnp.concatenate([a, b, a, c, b, a], axis=0)


def dot_nn(a, b):
    return lax.dot_general(a, b, (((1,), (0,)), ((), ())), preferred_element_type=F32)


def solve_kernel(
    g_ref, s_ref, basis_out, factor_out, a_ref, basis_ref, factor_ref, sems
):
    k = factor_ref.shape[0]
    copies = []
    row, col = square()
    mixed = g_ref[128:256]
    turned = mixed.T
    diag = [
        jnp.sum(jnp.where(row == col, mixed, 0.0), axis=0, keepdims=True),
        g_ref[256:257],
    ]
    right = [jnp.broadcast_to(lax.rsqrt(d), (128, 128)) for d in diag]
    left = [r.T for r in right]
    size = [jnp.sqrt(d) for d in diag]
    a_ref[:128, :128] = jnp.where(row >= col, mixed, turned) * left[0] * right[0]
    a_ref[:128, 128:k] = g_ref[0:128] * left[0] * right[1]
    last = jnp.where(row < col, mixed, turned)
    last = jnp.where(row == col, diag[1], last)
    a_ref[128:, 128:k] = last * left[1] * right[1]
    for j in range(s_ref.shape[1]):
        at = k + j * 128
        part = s_ref[:, j].reshape(k, 128)
        a_ref[:128, at : at + 128] = part[:128] * left[0]
        a_ref[128:, at : at + 128] = part[128:] * left[1]
    size = jnp.concatenate(size, axis=1)
    lane = lax.broadcasted_iota(jnp.int32, (NB, 128), 1)
    sub = lax.broadcasted_iota(jnp.int32, (NB, 128), 0)
    eye = jnp.where(lane == sub + NB, 1.0, 0.0)
    def send(i, src, dst, rows, first):
        copy = pltpu.make_async_copy(
            src.at[rows, :], dst.at[rows, :], sems.at[i, first // NB]
        )
        copy.start()
        copies.append(copy)

    def rest(first, twice):
        rows, at, after = slice(first, first + NB), first // 128 * 128, first + NB
        start = after // 128 * 128
        held = {}

        def begin():
            held["left"] = six_lanes(twice)

        def solve(c):
            x = dot_nn(held["left"], six_rows(a_ref[rows, c : c + 128]))
            held[c] = x
            if c >= k:
                basis_ref[rows, c - k : c - k + 128] = x
            else:
                col_id = c + lax.broadcasted_iota(jnp.int32, (NB, 128), 1)
                row_id = first + lax.broadcasted_iota(jnp.int32, (NB, 128), 0)
                factor_ref[rows, c : c + 128] = jnp.where(
                    col_id >= row_id, x * size[:, c : c + 128], 0.0
                )

        def leave():
            if at > 0:
                factor_ref[rows, :at] = jnp.zeros((NB, at), F32)
            send(0, basis_ref, basis_out, rows, first)
            send(1, factor_ref, factor_out, rows, first)

        def turn(c):
            x = jnp.concatenate([held[c], held[c]], axis=0).T
            held["turned", c] = six_lanes(x[max(after - c, 0) :])

        def update(c):
            left = jnp.concatenate(
                [held["turned", t] for t in range(start, k, 128)], axis=0
            )
            low = after + NB if c == start else after
            if low < k:
                a_ref[low:, c : c + 128] -= dot_nn(
                    left[low - after :], six_rows(held[c])
                )

        total = a_ref.shape[1]
        pieces = [begin]
        pieces += [functools.partial(solve, c) for c in range(at, total, 128)]
        pieces.append(leave)
        if after < k:
            pieces += [functools.partial(turn, c) for c in range(start, k, 128)]
            pieces += [functools.partial(update, c) for c in range(start, total, 128)]
        return pieces

    def ahead(first, twice):
        rows, after = slice(first, first + NB), first + NB
        start = after // 128 * 128
        x = dot_nn(six_lanes(twice), six_rows(a_ref[rows, start : start + 128]))
        turned = jnp.concatenate([x, x], axis=0).T
        turned = turned[after - start : after - start + NB]
        return a_ref[after : after + NB, start : start + 128] - dot_nn(
            six_lanes(turned), six_rows(x)
        )

    def keep(nxt, tile):
        at = nxt // 128 * 128
        a_ref[nxt : nxt + NB, at : at + 128] = tile

    aside = []
    for first in range(0, k, NB):
        at = first // 128 * 128
        if first == 0:
            tile = a_ref[0:NB, 0:128]
        elif first > at:
            tile = pltpu.roll(tile, NB, 1)
        u = factor_block(jnp.where(lane < NB, tile, eye), aside)
        twice = jnp.where(lane < NB, pltpu.roll(u, NB, 1), u)
        if first + NB < k:
            tile = ahead(first, twice)
            nxt = first + NB
            aside = rest(first, twice)
            aside.append(functools.partial(keep, nxt, tile))
    for piece in rest(k - NB, twice):
        piece()
    for copy in copies:
        copy.wait()


def orthonormalize(g, s):
    k = s.shape[0] * s.shape[2]
    n = s.shape[1] * 128
    return pl.pallas_call(
        solve_kernel,
        out_shape=(
            jax.ShapeDtypeStruct((k, n), F32),
            jax.ShapeDtypeStruct((k, k), F32),
        ),
        in_specs=[VMEM, VMEM],
        out_specs=(pl.BlockSpec(memory_space=pl.ANY),) * 2,
        scratch_shapes=[
            pltpu.VMEM((k, k + n), F32),
            pltpu.VMEM((k, n), F32),
            pltpu.VMEM((k, k), F32),
            pltpu.SemaphoreType.DMA((2, k // NB)),
        ],
        compiler_params=PARAMS,
        name="orthonormalize",
    )(near(g), near(s))


def sum_over_devices(packed):
    axes = ("row", "bundle")
    rows, bundles = lax.axis_size("row"), lax.axis_size("bundle")
    chips, planes = bundles // 2, 8
    line = rows // planes
    part = chips * line

    def device(z, y, x, core):
        return ((z * line + y) * chips + x) * 2 + core

    plane = [
        [device(z, y, x, core) for y in range(line) for x in range(chips)]
        for z in range(planes)
        for core in range(2)
    ]
    across = [
        [device(z, y, x, core) for z in range(planes) for core in range(2)]
        for y in range(line)
        for x in range(chips)
    ]

    def exchange(x, groups):
        return lax.all_to_all(
            x, axes, 0, 0, axis_index_groups=groups, tiled=True
        )

    def copies(x, n):
        return jnp.broadcast_to(x[None], (n,) + x.shape)

    mine = jnp.sum(exchange(packed.reshape(part, 1, -1), plane), axis=0)
    mine = jnp.sum(exchange(copies(mine, 2 * planes), across), axis=0)
    return exchange(copies(mine, part), plane).reshape(packed.shape)


def local(vectors, blocks, columns, bounds):
    block_rows = blocks.shape[0]
    row_count = lax.axis_size("row")
    bundles = lax.axis_size("bundle")
    total_rows = block_rows * row_count
    places = slot_places(
        columns, lax.axis_index("row"), block_rows, total_rows
    )
    inside = [(i, i ^ 1) for i in range(row_count)]
    outside = [
        (i, (i + 1 if i % 2 else i - 1) % row_count) for i in range(row_count)
    ]

    def sides(field):
        return (
            lax.ppermute(field, "row", inside),
            lax.ppermute(field, "row", outside),
        )

    inner, outer = sides(vectors)
    w = split_blocks(blocks)
    first = apply_step(
        0, places, bounds, vectors, inner, outer, None, w
    )
    inner, outer = sides(first)
    second = apply_step(
        1, places, bounds, first, inner, outer, vectors, w
    )
    inner, outer = sides(second)
    filtered = apply_step(
        2, places, bounds, second, inner, outer, first, w
    )
    tiles, width, lanes = filtered.shape
    stacked = lax.all_to_all(
        filtered.reshape(bundles, tiles // bundles, width, lanes),
        "bundle",
        split_axis=0,
        concat_axis=0,
        tiled=True,
    )
    gram = sum_over_devices(gram_packed(stacked))
    return orthonormalize(gram, stacked)


def solution(mesh):
    placed = (P("bundle", "row"), P("row", None, None), P("row", None), P())
    return jax.shard_map(
        local,
        mesh=mesh,
        in_specs=placed,
        out_specs=(P(None, ("row", "bundle")), P()),
        check_vma=False,
    )
```

```python
import functools

import jax
import jax.numpy as jnp
from jax import lax
from jax.experimental import pallas as pl
from jax.experimental.pallas import tpu as pltpu
from jax.sharding import PartitionSpec as P

BF = jnp.bfloat16
F32 = jnp.float32
HIGHEST = lax.Precision.HIGHEST
VMEM = pl.BlockSpec(memory_space=pltpu.VMEM)
SMEM = pl.BlockSpec(memory_space=pltpu.SMEM)
NB = 64
PACKED = 320
AHEAD = 8
PARAMS = pltpu.CompilerParams(vmem_limit_bytes=20 * 1024 * 1024)


def near(x):
    return pltpu.with_memory_space_constraint(x, pltpu.VMEM)


def split(x):
    hi = x.astype(BF)
    lo = (x - hi.astype(F32)).astype(BF)
    return hi, lo


def dot_nt(a, b):
    return lax.dot_general(a, b, (((1,), (1,)), ((), ())), preferred_element_type=F32)


def split_kernel(b_ref, w_ref):
    for i in range(b_ref.shape[0]):
        hi, lo = split(b_ref[i])
        both = jnp.concatenate([hi.astype(F32), lo.astype(F32)], axis=0)
        w_ref[i] = both.T.astype(BF)


def split_blocks(blocks):
    n, a, m = blocks.shape
    step = 8
    return pl.pallas_call(
        split_kernel,
        out_shape=pltpu.VMEM((n, m, 2 * a), BF),
        grid=(n // step,),
        in_specs=[pl.BlockSpec((step, a, m), lambda i: (i, 0, 0))],
        out_specs=pl.BlockSpec((step, m, 2 * a), lambda i: (i, 0, 0)),
        compiler_params=PARAMS,
        name="split_blocks",
    )(blocks)


def apply_kernel(stage, slot_ref, bounds_ref, *refs):
    if stage == 0:
        f_ref, inner_ref, outer_ref, w_ref, out_ref, e_ref = refs
        prev_ref = None
    else:
        f_ref, inner_ref, outer_ref, prev_ref, w_ref, out_ref, e_ref = refs
    width = f_ref.shape[0]
    tiles = f_ref.shape[1] // 128
    left = lax.broadcasted_iota(jnp.int32, (width, 128), 1) < 64
    left2 = lax.broadcasted_iota(jnp.int32, (2 * width, 128), 1) < 64

    def build(t):
        for part, ref in enumerate((inner_ref, f_ref, outer_ref)):
            x = ref[:, t * 128 : (t + 1) * 128]
            for v, y in enumerate((x, pltpu.roll(x, 64, 1))):
                hi, lo = split(y)
                at = (3 * v + part) * tiles + t
                e_ref[at, 0:width] = hi
                e_ref[at, width : 2 * width] = lo

    for t in range(tiles):
        build(t)

    center = (bounds_ref[0] + bounds_ref[1]) * 0.5
    half = (bounds_ref[1] - bounds_ref[0]) * 0.5
    slots = w_ref.shape[1] // 64

    def one(i):
        at = [slot_ref[i * slots + s] for s in range(slots)]
        lhs = jnp.concatenate(
            [
                jnp.where(left2, e_ref[at[s]], e_ref[at[s + 1]])
                for s in range(0, slots, 2)
            ],
            axis=1,
        )
        out = dot_nn(lhs, w_ref[i])
        acc = out[:width] + jnp.where(left, out[width:], 0.0)
        return acc + pltpu.roll(acc, 64, 1)

    def pair(g):
        y = jnp.where(left, one(2 * g), one(2 * g + 1))
        lanes = slice(g * 128, (g + 1) * 128)
        f = f_ref[:, lanes]
        r = (y - center * f) / half
        if stage > 0:
            r = 2.0 * r - prev_ref[:, lanes]
        if stage < 2:
            out_ref[:, lanes] = r
        else:
            out_ref[g] = r

    for g in range(tiles):
        pair(g)


def apply_step(stage, slot_table, bounds, f, inner, outer, prev, w):
    width, n = f.shape
    tiles = n // 128
    args = (f, inner, outer) + (() if prev is None else (prev,)) + (w,)
    out = (width, n) if stage < 2 else (tiles, width, 128)
    return pl.pallas_call(
        functools.partial(apply_kernel, stage),
        out_shape=pltpu.VMEM(out, F32),
        in_specs=[SMEM] * 2 + [VMEM] * len(args),
        out_specs=VMEM,
        scratch_shapes=[pltpu.VMEM((6 * tiles, 2 * width, 128), BF)],
        compiler_params=PARAMS,
        name=f"apply_{stage}",
    )(slot_table, bounds, *map(near, args))


def slot_places(columns, row, block_rows, total_rows):
    reach = jnp.mod(columns - (row - 1) * block_rows, total_rows)
    side, inner = reach // block_rows, reach % block_rows
    side = jnp.where(row % 2 == 0, 2 - side, side)
    right = jnp.arange(columns.shape[1], dtype=jnp.int32) % 2
    exchanged = (inner + right) % 2
    tiles = block_rows // 2
    return ((exchanged * 3 + side) * tiles + inner // 2).reshape(-1)


def square():
    return (
        lax.broadcasted_iota(jnp.int32, (128, 128), 0),
        lax.broadcasted_iota(jnp.int32, (128, 128), 1),
    )


def gram_kernel(s_ref, out_ref):
    s = jnp.concatenate(
        [
            s_ref[:, j].reshape(s_ref.shape[0] * s_ref.shape[2], 128)
            for j in range(s_ref.shape[1])
        ],
        axis=1,
    )
    g = lax.dot_general(
        s, s, (((1,), (1,)), ((), ())), precision=HIGHEST, preferred_element_type=F32
    )
    row, col = square()
    last = g[128:, 128:]
    out_ref[0:128] = g[:128, 128:]
    out_ref[128:256] = jnp.where(row >= col, g[:128, :128], last)
    out_ref[256:] = jnp.zeros((out_ref.shape[0] - 256, 128), F32)
    out_ref[256:257] = jnp.sum(
        jnp.where(row == col, last, 0.0), axis=0, keepdims=True
    )


def gram_packed(s):
    return pl.pallas_call(
        gram_kernel,
        out_shape=pltpu.VMEM((PACKED, 128), F32),
        in_specs=[VMEM],
        out_specs=VMEM,
        compiler_params=PARAMS,
        name="gram",
    )(near(s))


def row_of(x, r):
    return jnp.take_along_axis(x, jnp.full((8, 128), r, jnp.int32), axis=0)


def lane_of(x, c):
    return jnp.broadcast_to(x[:, c : c + 1], (8, 128))


def factor_block(m, aside=()):
    aside = list(aside)
    n = m.shape[0]
    sub = lax.broadcasted_iota(jnp.int32, (8, 128), 0)
    here = [sub == k for k in range(8)]
    vregs = [m[8 * v : 8 * v + 8] for v in range(n // 8)]
    done = []

    def update(some, v0, z):
        sums = {}
        for k in range(8):
            for v in some:
                t = lane_of(vregs[v], 8 * v0 + k) * z[k]
                sums[v] = sums[v] + t if k else t
        for v in some:
            vregs[v] = vregs[v] - sums[v]

    early = []
    for v0 in range(n // 8):
        head = vregs[v0]
        p = early + [lane_of(head, 8 * v0 + c) for c in range(len(early), 8)]
        more = AHEAD if v0 + 1 < n // 8 else 0
        p += [lane_of(head, 8 * v0 + 8 + c) for c in range(more)]
        out = jnp.zeros((8, 128), F32)
        for k in range(0, 8, 2):
            a, b, d = row_of(p[k], k), row_of(p[k + 1], k), row_of(p[k + 1], k + 1)
            det = a * d - b * b
            inv = 1.0 / det

            both = here[k] | here[k + 1]
            m0 = jnp.where(both, jnp.where(here[k], -1.0, 0.0), p[k])
            m1 = jnp.where(both, jnp.where(here[k + 1], -1.0, 0.0), p[k + 1])

            n0, n1 = m0 * d - m1 * b, m1 * a - m0 * b

            def eliminate(x):
                s0, s1 = row_of(x, k), row_of(x, k + 1)
                return jnp.where(both, 0.0, x) - (s0 * n0 + s1 * n1) * inv

            for c in range(k + 2, 8 + more):
                p[c] = eliminate(p[c])
            s0 = row_of(head, k)
            w1 = a * row_of(head, k + 1) - b * s0
            head = eliminate(head)
            out = jnp.where(here[k], s0 * lax.rsqrt(a), out)
            out = jnp.where(here[k + 1], w1 * lax.rsqrt(a * det), out)
        done.append(out)
        for _ in range(-(-len(aside) // max(1, n // 8 - 1 - v0))):
            aside.pop(0)()
        early = []
        for c in range(more):
            t = [
                lane_of(vregs[v0 + 1], 8 * v0 + k) * row_of(p[8 + c], k)
                for k in range(8)
            ]
            while len(t) > 1:
                t = [t[i] + t[i + 1] for i in range(0, len(t), 2)]
            early.append(lane_of(vregs[v0 + 1], 8 * v0 + 8 + c) - t[0])
        z = [row_of(head, k) for k in range(8)]
        for some in ([v0 + 1], list(range(v0 + 2, n // 8))):
            if some and some[0] < n // 8:
                update(some, v0, z)
    return jnp.concatenate(done, axis=0)


def split3(x):
    a = x.astype(BF)
    r = x - a.astype(F32)
    b = r.astype(BF)
    c = (r - b.astype(F32)).astype(BF)
    return a, b, c


def six_lanes(twice):
    a, b, c = split3(twice)
    left = lax.broadcasted_iota(jnp.int32, twice.shape, 1) < NB
    return jnp.concatenate([a, jnp.where(left, b, a), jnp.where(left, b, c)], axis=1)


def six_rows(x):
    a, b, c = split3(x)
    return jnp.concatenate([a, b, a, c, b, a], axis=0)


def dot_nn(a, b):
    return lax.dot_general(a, b, (((1,), (0,)), ((), ())), preferred_element_type=F32)


def solve_kernel(
    g_ref, s_ref, basis_out, factor_out, a_ref, basis_ref, factor_ref, sems
):
    k = factor_ref.shape[0]
    copies = []
    row, col = square()
    mixed = g_ref[128:256]
    turned = mixed.T
    diag = [
        jnp.sum(jnp.where(row == col, mixed, 0.0), axis=0, keepdims=True),
        g_ref[256:257],
    ]
    right = [jnp.broadcast_to(lax.rsqrt(d), (128, 128)) for d in diag]
    left = [r.T for r in right]
    size = [jnp.sqrt(d) for d in diag]
    a_ref[:128, :128] = jnp.where(row >= col, mixed, turned) * left[0] * right[0]
    a_ref[:128, 128:k] = g_ref[0:128] * left[0] * right[1]
    last = jnp.where(row < col, mixed, turned)
    last = jnp.where(row == col, diag[1], last)
    a_ref[128:, 128:k] = last * left[1] * right[1]
    for j in range(s_ref.shape[1]):
        at = k + j * 128
        part = s_ref[:, j].reshape(k, 128)
        a_ref[:128, at : at + 128] = part[:128] * left[0]
        a_ref[128:, at : at + 128] = part[128:] * left[1]
    size = jnp.concatenate(size, axis=1)
    lane = lax.broadcasted_iota(jnp.int32, (NB, 128), 1)
    sub = lax.broadcasted_iota(jnp.int32, (NB, 128), 0)
    eye = jnp.where(lane == sub + NB, 1.0, 0.0)
    def send(i, src, dst, rows, first):
        copy = pltpu.make_async_copy(
            src.at[rows, :], dst.at[rows, :], sems.at[i, first // NB]
        )
        copy.start()
        copies.append(copy)

    def rest(first, twice):
        rows, at, after = slice(first, first + NB), first // 128 * 128, first + NB
        start = after // 128 * 128
        held = {}

        def begin():
            held["left"] = six_lanes(twice)

        def solve(c):
            x = dot_nn(held["left"], six_rows(a_ref[rows, c : c + 128]))
            held[c] = x
            if c >= k:
                basis_ref[rows, c - k : c - k + 128] = x
            else:
                col_id = c + lax.broadcasted_iota(jnp.int32, (NB, 128), 1)
                row_id = first + lax.broadcasted_iota(jnp.int32, (NB, 128), 0)
                factor_ref[rows, c : c + 128] = jnp.where(
                    col_id >= row_id, x * size[:, c : c + 128], 0.0
                )

        def leave():
            if at > 0:
                factor_ref[rows, :at] = jnp.zeros((NB, at), F32)
            send(0, basis_ref, basis_out, rows, first)
            send(1, factor_ref, factor_out, rows, first)

        def turn(c):
            x = jnp.concatenate([held[c], held[c]], axis=0).T
            held["turned", c] = six_lanes(x[max(after - c, 0) :])

        def update(c):
            left = jnp.concatenate(
                [held["turned", t] for t in range(start, k, 128)], axis=0
            )
            low = after + NB if c == start else after
            if low < k:
                a_ref[low:, c : c + 128] -= dot_nn(
                    left[low - after :], six_rows(held[c])
                )

        total = a_ref.shape[1]
        pieces = [begin]
        pieces += [functools.partial(solve, c) for c in range(at, total, 128)]
        pieces.append(leave)
        if after < k:
            pieces += [functools.partial(turn, c) for c in range(start, k, 128)]
            pieces += [functools.partial(update, c) for c in range(start, total, 128)]
        return pieces

    def ahead(first, twice):
        rows, after = slice(first, first + NB), first + NB
        start = after // 128 * 128
        x = dot_nn(six_lanes(twice), six_rows(a_ref[rows, start : start + 128]))
        turned = jnp.concatenate([x, x], axis=0).T
        turned = turned[after - start : after - start + NB]
        return a_ref[after : after + NB, start : start + 128] - dot_nn(
            six_lanes(turned), six_rows(x)
        )

    def keep(nxt, tile):
        at = nxt // 128 * 128
        a_ref[nxt : nxt + NB, at : at + 128] = tile

    aside = []
    for first in range(0, k, NB):
        at = first // 128 * 128
        if first == 0:
            tile = a_ref[0:NB, 0:128]
        elif first > at:
            tile = pltpu.roll(tile, NB, 1)
        u = factor_block(jnp.where(lane < NB, tile, eye), aside)
        twice = jnp.where(lane < NB, pltpu.roll(u, NB, 1), u)
        if first + NB < k:
            tile = ahead(first, twice)
            nxt = first + NB
            aside = rest(first, twice)
            aside.append(functools.partial(keep, nxt, tile))
    for piece in rest(k - NB, twice):
        piece()
    for copy in copies:
        copy.wait()


def orthonormalize(g, s):
    k = s.shape[0] * s.shape[2]
    n = s.shape[1] * 128
    return pl.pallas_call(
        solve_kernel,
        out_shape=(
            jax.ShapeDtypeStruct((k, n), F32),
            jax.ShapeDtypeStruct((k, k), F32),
        ),
        in_specs=[VMEM, VMEM],
        out_specs=(pl.BlockSpec(memory_space=pl.ANY),) * 2,
        scratch_shapes=[
            pltpu.VMEM((k, k + n), F32),
            pltpu.VMEM((k, n), F32),
            pltpu.VMEM((k, k), F32),
            pltpu.SemaphoreType.DMA((2, k // NB)),
        ],
        compiler_params=PARAMS,
        name="orthonormalize",
    )(near(g), near(s))


def sum_over_devices(packed):
    axes = ("row", "bundle")
    rows, bundles = lax.axis_size("row"), lax.axis_size("bundle")
    chips, planes = bundles // 2, 8
    line = rows // planes
    part = chips * planes

    def device(z, y, x, core):
        return ((z * line + y) * chips + x) * 2 + core

    plane = [
        [device(z, y, x, core) for z in range(planes) for x in range(chips)]
        for y in range(line)
        for core in range(2)
    ]
    across = [
        [device(z, y, x, core) for y in range(line) for core in range(2)]
        for z in range(planes)
        for x in range(chips)
    ]

    def exchange(x, groups):
        return lax.all_to_all(
            x, axes, 0, 0, axis_index_groups=groups, tiled=True
        )

    def copies(x, n):
        return jnp.broadcast_to(x[None], (n,) + x.shape)

    mine = jnp.sum(exchange(packed.reshape(part, 1, -1), plane), axis=0)
    mine = jnp.sum(exchange(copies(mine, 2 * line), across), axis=0)
    return exchange(copies(mine, part), plane).reshape(packed.shape)


def local(vectors, blocks, columns, bounds):
    block_rows = blocks.shape[0]
    row_count = lax.axis_size("row")
    bundles = lax.axis_size("bundle")
    total_rows = block_rows * row_count
    places = slot_places(
        columns, lax.axis_index("row"), block_rows, total_rows
    )
    inside = [(i, i ^ 1) for i in range(row_count)]
    outside = [
        (i, (i + 1 if i % 2 else i - 1) % row_count) for i in range(row_count)
    ]

    def sides(field):
        return (
            lax.ppermute(field, "row", inside),
            lax.ppermute(field, "row", outside),
        )

    inner, outer = sides(vectors)
    w = split_blocks(blocks)
    first = apply_step(
        0, places, bounds, vectors, inner, outer, None, w
    )
    inner, outer = sides(first)
    second = apply_step(
        1, places, bounds, first, inner, outer, vectors, w
    )
    inner, outer = sides(second)
    filtered = apply_step(
        2, places, bounds, second, inner, outer, first, w
    )
    tiles, width, lanes = filtered.shape
    stacked = lax.all_to_all(
        filtered.reshape(bundles, tiles // bundles, width, lanes),
        "bundle",
        split_axis=0,
        concat_axis=0,
        tiled=True,
    )
    gram = sum_over_devices(gram_packed(stacked))
    return orthonormalize(gram, stacked)


def solution(mesh):
    placed = (P("bundle", "row"), P("row", None, None), P("row", None), P())
    return jax.shard_map(
        local,
        mesh=mesh,
        in_specs=placed,
        out_specs=(P(None, ("row", "bundle")), P()),
        check_vma=False,
    )
```
